128 devices in a mesh: psg: 32 (over y, z, core), qry: 4 (over x).
Axes of the slice: x: 4, y: 4, z: 4, core: 2. Of those that a mesh axis runs over, the one named last changes fastest.
Arguments:
- queries: bfloat16 [512, 32, 128], P(('psg', 'qry')), may hold values from -6 to 6
- passages: bfloat16 [1024, 256, 128], P('psg'), may hold values from -6 to 6
- candidates: int32 [512, 32], P(('psg', 'qry')), may hold values from 0 to 1023, as said below
- teacher: float32 [512, 32], P(('psg', 'qry')), may hold values from -8 to 8
Outputs:
- pair_loss: float32 [512], P(('psg', 'qry'))
- grad_queries: bfloat16 [512, 32, 128], P(('psg', 'qry'))
- grad_passages: bfloat16 [1024, 256, 128], P('psg', 'qry')
The draws below stay inside these ranges and needn't reach their ends.
Inputs may be any that keep to these rules, and one draw needn't show every extreme that they name: Passage p lies in block p // 32. Among the 4 x 32 candidates of one device's queries (aligned blocks of 4 rows), at most 10 lie in one passage block; one passage block, the same for all devices, holds exactly 10 of every device's candidates. Candidate ids of one query may repeat.
All inputs are finite; a program needn't handle non-finite values.
Results may differ from the reference program's by a relative error of at most 0.019.
Values may be sent and summed in bfloat16 or wider, within the bound.
A program may use at most 64 MiB of HBM per device.

```python
import jax
import jax.numpy as jnp
from jax import lax

E = 128
QT = 32
PT = 256
C = 32
QD = 4
PS_DEV = 32
NQ = 512
NP = 1024
CAP = 10
N_QRY = 4


def draw_candidates(key, part):
    blocks = NQ // QD
    owners = NP // PS_DEV
    pair_count = QD * C
    slot_count = owners * CAP
    hottest = jax.random.randint(jax.random.fold_in(key, 11), (), 0, owners)

    def one_block(block_key):
        subkeys = jax.random.split(block_key, 4)
        ranking = jax.random.permutation(subkeys[0], owners)
        slot_owner = jnp.arange(slot_count) // CAP
        owner_rank = ranking[slot_owner]
        jitter = jax.random.randint(subkeys[1], (slot_count,), 0, 4096)
        precedence_rank = jitter + (owners - 1 - owner_rank) * (8192 // owners)
        precedence_rank = jnp.where(slot_owner == hottest, 16384, precedence_rank)
        distinct = precedence_rank * 8192 + jnp.arange(slot_count)
        picked = jnp.argsort(-distinct, stable=True)[:pair_count]
        picked = jax.random.permutation(subkeys[2], picked)
        local_ids = jax.random.randint(subkeys[3], (pair_count,), 0, PS_DEV)
        return (picked // CAP * PS_DEV + local_ids).reshape(QD, C).astype(jnp.int32)
    result = jax.vmap(one_block)(jax.random.split(jax.random.fold_in(key, 7), blocks))
    return result.reshape(NQ, C).astype(jnp.int32)


def steps_of(rng, dims, cuts, low, top_value):
    level, own = 1.0, jax.random.fold_in(rng, 6)
    for dim, shards_of in cuts:
        heights = jnp.exp(jax.random.uniform(jax.random.fold_in(own, dim), (shards_of,), jnp.float32, low / len(cuts), top_value / len(cuts)))
        level = level * jnp.repeat(heights, dims[dim] // shards_of).reshape([-1 if axis == dim else 1 for axis in range(len(dims))])
    return level


def normal_values(own_key, dims, deviation, bound, cuts=(), dtype=jnp.bfloat16):
    values = deviation * jax.random.normal(own_key, dims, jnp.float32)
    if cuts:
        values = values * steps_of(own_key, dims, cuts, -0.22, 0.18)
    return jnp.clip(values, -bound, bound).astype(dtype)


def setup_inputs(seed: int = 0) -> dict:
    key_of = jax.random.split(jax.random.key(seed), 5)
    queries = normal_values(key_of[0], (NQ, QT, E), 1.0, 6.0, ((0, 128),))
    passages = normal_values(key_of[1], (NP, PT, E), 1.0, 6.0, ((0, 32),))
    candidates = draw_candidates(jax.random.fold_in(key_of[4], 71), 0)
    teacher = normal_values(key_of[3], (NQ, C), 2.0, 8.0, ((0, 128),), jnp.float32)
    return {"queries": queries, "passages": passages, "candidates": candidates, "teacher": teacher}


epsilon = 1e-06
softness_scale = 0.05

def normalize(values):
    widened = values.astype(jnp.float32)
    inverse_norm = lax.rsqrt(lax.optimization_barrier(jnp.sum(widened * widened, -1, keepdims=True)) + epsilon)
    return (widened * inverse_norm, inverse_norm)

def token_terms(passage_norm, query_row, passage_ids):
    gathered = jnp.take(passage_norm, passage_ids, axis=0).astype(jnp.float32)
    token_products = jnp.einsum('qe,cpe->cqp', query_row.astype(jnp.float32), gathered)
    power_value = jnp.exp(token_products / softness_scale)
    return (gathered, power_value, lax.optimization_barrier(jnp.sum(power_value, -1)))

def take_shard(values, shard):
    group_count = NQ // (QD * N_QRY)
    shaped = values.reshape((group_count, N_QRY, QD) + values.shape[1:])
    return shaped[:, shard].reshape((group_count * QD,) + values.shape[1:])

def reference(queries, passages, candidates, teacher):
    query_unit, query_inverse = normalize(queries)
    passage_unit, passage_inverse = normalize(passages)
    query_norm = query_unit.astype(jnp.bfloat16)
    passage_norm = passage_unit.astype(jnp.bfloat16)

    def score_one(element):
        reduced_sum = token_terms(passage_norm, element[0], element[1])[2]
        return lax.optimization_barrier(jnp.sum(softness_scale * jnp.log(reduced_sum), -1))
    scores = lax.map(score_one, (query_norm, candidates))
    teacher_exp = jnp.exp(teacher)
    mentor_score_sum = lax.optimization_barrier(jnp.sum(teacher_exp, -1, keepdims=True))
    target = teacher_exp / mentor_score_sum
    log_target = teacher - jnp.log(mentor_score_sum)
    score_exp = jnp.exp(scores)
    score_total = lax.optimization_barrier(jnp.sum(score_exp, -1, keepdims=True))
    likelihood = score_exp / score_total
    pair_loss = lax.optimization_barrier(jnp.sum(target * (log_target - scores), -1)) + jnp.log(score_total[:, 0])
    score_grad = likelihood - target
    group_count = NQ // (QD * N_QRY)
    query_parts = []
    unit_passage_grad = jnp.zeros((NP, PT, E), jnp.float32)
    for shard in range(N_QRY):

        def step(running, element):
            query_row, passage_ids, grad_row = element
            gathered, power_value, reduced_sum = token_terms(passage_norm, query_row, passage_ids)
            weights = (grad_row[:, None, None] * power_value / reduced_sum[:, :, None]).astype(jnp.bfloat16)
            weights = lax.optimization_barrier(weights).astype(jnp.float32)
            query_delta = jnp.einsum('cqp,cpe->qe', weights, gathered)
            pair_grads = jnp.einsum('cqp,qe->cpe', weights, query_row.astype(jnp.float32))
            return (running.at[passage_ids].add(pair_grads), query_delta)
        partial_value, query_grads = lax.scan(step, jnp.zeros((NP, PT, E), jnp.float32), (take_shard(query_norm, shard), take_shard(candidates, shard), take_shard(score_grad, shard)))
        rounded = lax.optimization_barrier(partial_value.astype(jnp.bfloat16))
        unit_passage_grad = unit_passage_grad + rounded.astype(jnp.float32)
        query_parts.append(query_grads.reshape(group_count, QD, QT, E))
    unit_query_grad = jnp.stack(query_parts, 1).reshape(NQ, QT, E)
    grad_queries = query_inverse * (unit_query_grad - query_unit * lax.optimization_barrier(jnp.sum(query_unit * unit_query_grad, -1, keepdims=True)))
    grad_passages = passage_inverse * (unit_passage_grad - passage_unit * lax.optimization_barrier(jnp.sum(passage_unit * unit_passage_grad, -1, keepdims=True)))
    return (pair_loss, grad_queries.astype(jnp.bfloat16), grad_passages.astype(jnp.bfloat16))
```

```python
import math

import jax
import jax.numpy as jnp
from jax import lax
from jax.experimental import pallas as pl
from jax.experimental.pallas import tpu as pltpu
from jax.sharding import PartitionSpec as P

MESH = pl.DeviceIdType.MESH
BF16, F32, I32 = jnp.bfloat16, jnp.float32, jnp.int32
HIGHEST = lax.Precision.HIGHEST
epsilon = 1e-06
softness_scale = 0.05

OWNERS, GROUPS, CHIPS = 32, 4, 16
QD, QT, C, E, PT, PS = 4, 32, 32, 128, 256, 32
CAP = 10
ROW = QD * QT
SHARE = PT // GROUPS
PER_CHUNK = 4
CHUNKS = (OWNERS * CAP + PS * (PER_CHUNK - 1)) // PER_CHUNK
UNROLL = 4
STEPS = CHUNKS // UNROLL
SLOTS = 512
LANES_PER_SENDER = SLOTS // OWNERS
ORDER = (2, 1, 3, 0)

NT = (((1,), (1,)), ((), ()))
TN = (((0,), (0,)), ((), ()))


def iota(shape, dim):
    return lax.broadcasted_iota(I32, shape, dim)


def dot(a, b, dims=None, precision=None):
    dims = (((1,), (0,)), ((), ())) if dims is None else dims
    return lax.dot_general(a, b, dims, precision=precision, preferred_element_type=F32)


def unit_of(values):
    inverse = lax.rsqrt(jnp.sum(values * values, -1, keepdims=True) + epsilon)
    return values * inverse, inverse


def project(values, gradient):
    unit, inverse = unit_of(values)
    return inverse * (gradient - unit * jnp.sum(unit * gradient, -1, keepdims=True))


def count(mask, axis):
    return jnp.sum(jnp.where(mask, 1, 0), axis, keepdims=True)


def same(a, b):
    return (1 - jnp.minimum((a - b) * (a - b), 1)).astype(F32)


def column_of(row):
    return jnp.broadcast_to(row, (ROW, row.shape[1])).T[:, 0:1]


def slot_tables(ids, teacher):
    lane = iota((1, ROW), 1)
    power = jnp.exp(teacher)
    same_query = (iota((ROW, ROW), 0) // C == iota((ROW, ROW), 1) // C).astype(F32)
    power_sum = dot(jnp.broadcast_to(power, (8, ROW)), same_query, precision=HIGHEST)[0:1]
    target = power / power_sum
    owner = ids >> 5
    code = (lane >> 5) * PS + (ids & (PS - 1)) + 1
    ahead = iota((ROW, ROW), 0) < iota((ROW, ROW), 1)
    rank = count((column_of(owner) == owner) & ahead, 0)
    hits = owner == iota((OWNERS, ROW), 0)
    place = iota((OWNERS, ROW), 1) & (LANES_PER_SENDER - 1)
    codes = jnp.zeros((OWNERS, ROW), I32)
    targets = jnp.zeros((OWNERS, ROW), F32)
    for slot in range(CAP):
        chosen = hits & (rank == slot)
        codes = jnp.where(place == slot, jnp.sum(jnp.where(chosen, code, 0), 1, keepdims=True), codes)
        targets = jnp.where(place == slot, jnp.sum(jnp.where(chosen, target, 0.0), 1, keepdims=True), targets)
    return codes, targets


def order_slots(codes, targets):
    lane = iota((OWNERS, SLOTS), 1)
    mine = lane >> 4 == iota((OWNERS, SLOTS), 0)
    code = jnp.sum(jnp.where(mine, jnp.concatenate([codes] * 4, 1), 0), 0, keepdims=True) - 1
    target = jnp.sum(jnp.where(mine, jnp.concatenate([targets] * 4, 1), 0.0), 0, keepdims=True)
    live = code >= 0
    local = code >> 5
    query = (iota((1, SLOTS), 1) >> 4) * QD + local
    passage = jnp.where(live, code & (PS - 1), -1)
    ahead = iota((SLOTS, SLOTS), 0) < iota((SLOTS, SLOTS), 1)
    rank = count((column_of(passage) == passage) & ahead, 0)
    index = iota((PS, SLOTS), 0)
    hits = passage == index
    chunks = (count(hits, 1) + (PER_CHUNK - 1)) >> 2
    chunk_row = jnp.sum(jnp.where(lane == index, chunks, 0), 0, keepdims=True)
    first = jnp.sum(jnp.where(lane < index, chunk_row, 0), 1, keepdims=True)
    place = rank + PER_CHUNK * jnp.sum(jnp.where(hits, first, 0), 0, keepdims=True)
    place = jnp.where(live, place, -1)
    ordered = column_of(place) == iota((SLOTS, SLOTS), 1)
    ordered = jnp.sum(jnp.where(ordered, column_of(query) + 1, 0), 0, keepdims=True) - 1
    inside = (first <= lane) & (lane < first + chunks)
    chunk_passage = jnp.sum(jnp.where(inside, index, 0), 0, keepdims=True)
    last = jnp.where(lane == index, jnp.maximum(first + chunks - 1, 0), 0)
    last = jnp.where(lane == index + ROW, jnp.minimum(chunks, 1), last)
    meta = [
        jnp.maximum(ordered, 0),
        chunk_passage,
        jnp.maximum(place, 0),
        jnp.where(live, local, -1),
        jnp.sum(last, 0, keepdims=True),
        ordered,
    ]
    chosen = (iota((SLOTS, SLOTS), 0) == place).astype(BF16)
    high = target.astype(BF16).astype(F32)
    middle = (target - high).astype(BF16).astype(F32)
    low = target - high - middle
    pick = iota((ROW, SLOTS), 0)
    values = jnp.zeros((ROW, SLOTS), F32)
    for row_index, row in enumerate((query.astype(F32), live.astype(F32), high, middle, low)):
        values = jnp.where(pick == row_index, row, values)
    return meta, dot(chosen, values.astype(BF16), NT)


def kernel(
    q_ref, ids_ref, teacher_ref, passages_hbm,
    total_out, gq_out, gp_out,
    q_all, raw, p_norm, code_out, code_in, target_out, target_in, meta_v, meta_s, column, exps_a, exps_b, terms, scaled,
    scores, grads, sums_out, sums_in, part_a, part_b, r2, r1, r3, in_left, in_right, from_left, from_right,
    g_sib_out, g_sib_in, g_out, g_in,
    local_sem, q_send, q_recv, relay_send, relay_recv, code_send, code_recv, target_send, target_recv,
    sums_send, sums_recv, x_send, x_recv, sib_send, sib_recv, g_send, g_recv,
):
    me = lax.axis_index("psg")
    col = lax.axis_index("qry")
    chip, core = me // 2, me % 2
    sibling = chip * 2 + (1 - core)
    right, left = (col + 1) % GROUPS, (col + GROUPS - 1) % GROUPS

    def peer(step):
        return (me + step) % OWNERS

    barrier = pltpu.get_barrier_semaphore()

    def greet(step, carry):
        pl.semaphore_signal(barrier, inc=1, device_id={"psg": peer(step)}, device_id_type=MESH)
        return carry

    lax.fori_loop(1, OWNERS, greet, 0)
    for side in (left, right):
        pl.semaphore_signal(barrier, inc=1, device_id={"qry": side}, device_id_type=MESH)

    loads = []
    for index, relative in enumerate(ORDER):
        share = (col + relative) % GROUPS
        load = pltpu.make_async_copy(
            passages_hbm.at[:, pl.ds(pl.multiple_of(share * SHARE, SHARE), SHARE), :],
            raw.at[:, pl.ds(index * SHARE, SHARE), :],
            local_sem.at[index],
        )
        load.start()
        loads.append(load)

    q_raw = q_ref[...].astype(F32)
    own_rows = pl.ds(me * QD, QD)
    q_all[own_rows] = unit_of(q_raw)[0].astype(BF16).reshape(QD, QT, E)
    codes, targets = slot_tables(ids_ref[...], teacher_ref[...])
    for owner in range(OWNERS):
        code_out[owner] = codes[owner : owner + 1]
        target_out[owner] = targets[owner : owner + 1]
    code_in[me] = code_out[me]
    target_in[me] = target_out[me]

    pl.semaphore_wait(barrier, OWNERS - 1 + 2)

    def send_table(step, carry):
        pltpu.make_async_remote_copy(
            src_ref=code_out.at[peer(step)], dst_ref=code_in.at[me], send_sem=code_send, recv_sem=code_recv,
            device_id={"psg": peer(step)}, device_id_type=MESH,
        ).start()
        pltpu.make_async_remote_copy(
            src_ref=target_out.at[peer(step)], dst_ref=target_in.at[me], send_sem=target_send, recv_sem=target_recv,
            device_id={"psg": peer(step)}, device_id_type=MESH,
        ).start()
        return carry

    lax.fori_loop(1, OWNERS, send_table, 0)

    def send_query(step, carry):
        pltpu.make_async_remote_copy(
            src_ref=q_all.at[own_rows], dst_ref=q_all.at[own_rows], send_sem=q_send, recv_sem=q_recv.at[chip],
            device_id={"psg": ((chip + step) % CHIPS) * 2 + core}, device_id_type=MESH,
        ).start()
        return carry

    lax.fori_loop(1, CHIPS, send_query, 0)

    def relay(rows):
        return pltpu.make_async_remote_copy(
            src_ref=q_all.at[rows], dst_ref=q_all.at[rows], send_sem=relay_send, recv_sem=relay_recv,
            device_id={"psg": sibling}, device_id_type=MESH,
        )

    relay(own_rows).start()

    for load in loads:
        load.wait()

    def normalize(index, carry):
        values = raw[index].astype(F32)
        p_norm[index] = unit_of(values)[0].astype(BF16)
        return carry

    lax.fori_loop(0, PS, normalize, 0, unroll=4)

    others = pl.ds(0, OWNERS - 1)
    pltpu.make_async_copy(code_in.at[others], code_in.at[others], code_recv).wait()
    pltpu.make_async_copy(target_in.at[others], target_in.at[others], target_recv).wait()
    meta, by_column = order_slots(
        jnp.concatenate([code_in[owner] for owner in range(OWNERS)], 0),
        jnp.concatenate([target_in[owner] for owner in range(OWNERS)], 0),
    )
    for index, row in enumerate(meta):
        meta_v[index : index + 1, :] = row
    meta_v[6:8, :] = jnp.zeros((2, SLOTS), I32)
    column[...] = by_column
    scores[...] = jnp.zeros_like(scores)

    def hand_on(step, carry):
        sender = (chip + CHIPS - step) % CHIPS
        rows = pl.ds((sender * 2 + core) * QD, QD)
        pltpu.make_async_copy(q_all.at[rows], q_all.at[rows], q_recv.at[sender]).wait()
        relay(rows).start()
        return carry

    lax.fori_loop(1, CHIPS, hand_on, 0)
    to_scalar = pltpu.make_async_copy(meta_v, meta_s, local_sem.at[4])
    to_scalar.start()
    to_scalar.wait()
    half = pl.ds(0, CHIPS * QD)
    pltpu.make_async_copy(q_all.at[half], q_all.at[half], relay_recv).wait()

    factor = math.log2(math.e) / softness_scale
    ones = jnp.ones((PT, E), BF16)

    def forward(step, carry):
        lines = []
        for inner in range(UNROLL):
            chunk = step * UNROLL + inner
            rows = pl.ds(pl.multiple_of(chunk * ROW, ROW), ROW)
            passage = meta_s[1, chunk]
            tokens = p_norm[passage]
            queries = jnp.concatenate(
                [
                    q_all[meta_s[0, chunk * PER_CHUNK + slot]]
                    for slot in range(PER_CHUNK)
                ],
                0,
            )
            power = jnp.exp2(dot(queries, tokens, NT) * factor).astype(BF16)
            exps_a[rows, :] = power[:, : PT // 2]
            exps_b[rows, :] = power[:, PT // 2 :]
            both = dot(power, jnp.concatenate([tokens, ones], 1))
            total = both[:, E:]
            inverse = 1.0 / total
            terms[pl.ds(chunk * PER_CHUNK, PER_CHUNK)] = (
                (both[:, :E] * inverse).astype(BF16).reshape(PER_CHUNK, QT, E)
            )
            scaled[rows, :] = (queries.astype(F32) * inverse).astype(BF16)
            logs = jnp.log(total)
            for slot in range(PER_CHUNK):
                lines.append(jnp.sum(logs[slot * QT : (slot + 1) * QT], 0, keepdims=True))
        line_count = UNROLL * PER_CHUNK
        lines = jnp.concatenate(lines, 0) * softness_scale
        scores[pl.ds(pl.multiple_of(step * line_count, line_count), line_count), :] = lines
        return carry

    lax.fori_loop(0, STEPS, forward, 0)

    query_row = meta_v[5:6, :]
    live = column[:, 1:2] > 0.5
    target = column[:, 2:3] + column[:, 3:4] + column[:, 4:5]
    score = scores[...]
    power = jnp.exp(score)
    lane = iota((SLOTS, ROW), 1)
    summands = jnp.where(live, jnp.where(lane < ROW // 2, power, target * score), 0.0)
    belongs = (query_row == iota((ROW, SLOTS), 0)).astype(F32)
    partial = dot(belongs, summands, precision=HIGHEST).T
    sums_out[0:1, :] = partial[0:1]
    sums_out[1:2, :] = partial[ROW // 2 : ROW // 2 + 1]
    sums_in[me] = sums_out[...]

    def send_sums(step, carry):
        pltpu.make_async_remote_copy(
            src_ref=sums_out, dst_ref=sums_in.at[me], send_sem=sums_send, recv_sem=sums_recv,
            device_id={"psg": peer(step)}, device_id_type=MESH,
        ).start()
        return carry

    lax.fori_loop(1, OWNERS, send_sums, 0)
    pltpu.make_async_copy(sums_in.at[others], sums_in.at[others], sums_recv).wait()
    totals = sums_in[0]
    for owner in range(1, OWNERS):
        totals = totals + sums_in[owner]
    total_row = totals[0:1]
    total_out[...] = jnp.log(total_row) - totals[1:2]
    own_query = column[:, 0:1].astype(I32) == lane
    total_here = jnp.sum(jnp.where(own_query, total_row, 0.0), 1, keepdims=True)
    grads[...] = jnp.where(live, power / jnp.where(live, total_here, 1.0) - target, 0.0)

    def passage_step(first, exps, parts):
        def run(step, running):
            line_count = UNROLL * PER_CHUNK
            grad_rows = grads[pl.ds(pl.multiple_of(step * line_count, line_count), line_count), :] if first else None
            for inner in range(UNROLL):
                chunk = step * UNROLL + inner
                rows = pl.ds(pl.multiple_of(chunk * ROW, ROW), ROW)
                here = meta_s[1, chunk]
                before = meta_s[1, jnp.maximum(chunk - 1, 0)]
                keep = same(here, before)
                if first:
                    weight = jnp.concatenate(
                        [
                            jnp.broadcast_to(grad_rows[inner * PER_CHUNK + slot][None, :], (QT, E))
                            for slot in range(PER_CHUNK)
                        ],
                        0,
                    )
                    side = (scaled[rows, :].astype(F32) * weight).astype(BF16)
                    scaled[rows, :] = side
                else:
                    side = scaled[rows, :]
                running = running * keep + dot(exps[rows, :], side, TN)
                parts[chunk] = running.astype(BF16)
            return running

        lax.fori_loop(0, STEPS, run, jnp.zeros((2 * SHARE, E), F32))

    def last_part(parts, index, begin):
        used = meta_s[4, ROW + index].astype(F32)
        return parts[meta_s[4, index]][begin : begin + SHARE].astype(F32) * used

    def collect(parts, begin, out):
        def run(index, carry):
            out[index] = last_part(parts, index, begin).astype(BF16)
            return carry

        lax.fori_loop(0, PS, run, 0, unroll=4)

    def send_x(index, side, source, target_ref):
        copy = pltpu.make_async_remote_copy(
            src_ref=source, dst_ref=target_ref, send_sem=x_send.at[index], recv_sem=x_recv.at[index],
            device_id={"qry": side}, device_id_type=MESH,
        )
        copy.start()
        return copy

    low, high = pl.ds(0, PS // 2), pl.ds(PS // 2, PS // 2)
    passage_step(True, exps_a, part_a)
    collect(part_a, 0, r2)
    onward_right = send_x(0, right, r2.at[low], in_left)
    onward_left = send_x(1, left, r2.at[high], in_right)
    collect(part_a, SHARE, r1)
    direct_right = send_x(2, right, r1.at[high], from_left.at[high])
    passage_step(False, exps_b, part_b)
    collect(part_b, 0, r3)
    direct_left = send_x(3, left, r3.at[low], from_right.at[low])

    def query_block(sender):
        sums = [jnp.zeros((QT, E), F32) for _ in range(QD)]
        for slot in range(CAP):
            index = sender * LANES_PER_SENDER + slot
            place = meta_s[2, index]
            local = meta_s[3, index]
            term = terms[place].astype(F32) * grads[pl.ds(place, 1), :]
            for query in range(QD):
                sums[query] = sums[query] + term * same(local, query)
        return jnp.concatenate(sums, 0)

    def for_sibling(index, carry):
        g_sib_out[index] = query_block(index * 2 + (1 - core)).astype(BF16)
        return carry

    def for_chips(index, carry):
        g_out[index] = query_block(index * 2 + core).astype(BF16)
        return carry

    lax.fori_loop(0, CHIPS, for_sibling, 0)
    to_sibling = pltpu.make_async_remote_copy(
        src_ref=g_sib_out, dst_ref=g_sib_in, send_sem=sib_send, recv_sem=sib_recv,
        device_id={"psg": sibling}, device_id_type=MESH,
    )
    to_sibling.start()
    lax.fori_loop(0, CHIPS, for_chips, 0)
    to_sibling.wait_recv()

    def add_sibling(index, carry):
        g_out[index] = (g_out[index].astype(F32) + g_sib_in[index].astype(F32)).astype(BF16)
        return carry

    lax.fori_loop(0, CHIPS, add_sibling, 0)

    def send_grad(step, carry):
        other = (chip + step) % CHIPS
        pltpu.make_async_remote_copy(
            src_ref=g_out.at[other], dst_ref=g_in.at[chip], send_sem=g_send, recv_sem=g_recv,
            device_id={"psg": other * 2 + core}, device_id_type=MESH,
        ).start()
        return carry

    lax.fori_loop(1, CHIPS, send_grad, 0)
    g_in[chip] = g_out[chip]

    def merge(incoming, out, begin):
        def run(index, carry):
            both = out[begin + index].astype(F32) + incoming[index].astype(F32)
            out[begin + index] = both.astype(BF16)
            return carry

        lax.fori_loop(0, PS // 2, run, 0, unroll=4)

    onward_right.wait_recv()
    merge(in_left, r1, 0)
    final_right = send_x(4, right, r1.at[low], from_left.at[low])
    onward_left.wait_recv()
    merge(in_right, r3, PS // 2)
    final_left = send_x(5, left, r3.at[high], from_right.at[high])

    fewer = pl.ds(0, CHIPS - 1)
    pltpu.make_async_copy(g_in.at[fewer], g_in.at[fewer], g_recv).wait()
    gradient = jnp.zeros((ROW, E), F32)
    for index in range(CHIPS):
        gradient = gradient + g_in[index].astype(F32)
    gq_out[...] = project(q_ref[...].astype(F32), gradient).astype(BF16)

    for copy in (direct_right, direct_left, final_right, final_left):
        copy.wait_recv()

    def finish(index, carry):
        gradient = last_part(part_b, index, SHARE)
        gradient = gradient + from_left[index].astype(F32) + from_right[index].astype(F32)
        values = raw[index, 3 * SHARE : 4 * SHARE, :].astype(F32)
        gp_out[index] = project(values, gradient).astype(BF16)
        return carry

    lax.fori_loop(0, PS, finish, 0, unroll=4)

    for copy in (onward_right, onward_left, direct_right, direct_left, final_right, final_left, to_sibling):
        copy.wait_send()
    pltpu.make_async_copy(code_in.at[others], code_in.at[others], code_send).wait()
    pltpu.make_async_copy(target_in.at[others], target_in.at[others], target_send).wait()
    pltpu.make_async_copy(sums_in.at[others], sums_in.at[others], sums_send).wait()
    pltpu.make_async_copy(g_in.at[fewer], g_in.at[fewer], g_send).wait()
    sent = pl.ds(0, (CHIPS - 1) * QD)
    pltpu.make_async_copy(q_all.at[sent], q_all.at[sent], q_send).wait()
    pltpu.make_async_copy(q_all.at[half], q_all.at[half], relay_send).wait()


def step(queries, ids, teacher, passages):
    dma = pltpu.SemaphoreType.DMA
    vmem = pltpu.VMEM
    rows = CHUNKS * ROW
    share = (PS, SHARE, E)
    half_share = (PS // 2, SHARE, E)
    return pl.pallas_call(
        kernel,
        out_shape=(
            jax.ShapeDtypeStruct((1, ROW), F32),
            jax.ShapeDtypeStruct((ROW, E), BF16),
            jax.ShapeDtypeStruct(share, BF16),
        ),
        in_specs=[pl.BlockSpec(memory_space=pltpu.VMEM)] * 3 + [pl.BlockSpec(memory_space=pl.ANY)],
        out_specs=(pl.BlockSpec(memory_space=pltpu.VMEM),) * 3,
        scratch_shapes=[
            vmem((OWNERS * QD, QT, E), BF16),
            vmem((PS, PT, E), BF16),
            vmem((PS, PT, E), BF16),
            vmem((OWNERS, 1, ROW), I32),
            vmem((OWNERS, 1, ROW), I32),
            vmem((OWNERS, 1, ROW), F32),
            vmem((OWNERS, 1, ROW), F32),
            vmem((8, SLOTS), I32),
            pltpu.SMEM((8, SLOTS), I32),
            vmem((SLOTS, ROW), F32),
            vmem((rows, PT // 2), BF16),
            vmem((rows, PT // 2), BF16),
            vmem((CHUNKS * PER_CHUNK, QT, E), BF16),
            vmem((rows, E), BF16),
            vmem((SLOTS, ROW), F32),
            vmem((SLOTS, ROW), F32),
            vmem((2, ROW), F32),
            vmem((OWNERS, 2, ROW), F32),
            vmem((CHUNKS, 2 * SHARE, E), BF16),
            vmem((CHUNKS, 2 * SHARE, E), BF16),
            vmem(share, BF16),
            vmem(share, BF16),
            vmem(share, BF16),
            vmem(half_share, BF16),
            vmem(half_share, BF16),
            vmem(share, BF16),
            vmem(share, BF16),
            vmem((CHIPS, ROW, E), BF16),
            vmem((CHIPS, ROW, E), BF16),
            vmem((CHIPS, ROW, E), BF16),
            vmem((CHIPS, ROW, E), BF16),
            dma((5,)),
            dma,
            dma((CHIPS,)),
            dma,
            dma,
            dma,
            dma,
            dma,
            dma,
            dma,
            dma,
            dma((6,)),
            dma((6,)),
            dma,
            dma,
            dma,
            dma,
        ],
        compiler_params=pltpu.CompilerParams(collective_id=0, has_side_effects=True),
    )(queries, ids, teacher, passages)


def shards(queries, passages, candidates, teacher):
    teacher_exp = jnp.exp(teacher)
    teacher_sum = jnp.sum(teacher_exp, -1, keepdims=True)
    entropy = jnp.sum(teacher_exp / teacher_sum * (teacher - jnp.log(teacher_sum)), -1)
    total_terms, grad_queries, grad_passages = step(
        queries.reshape(ROW, E), candidates.reshape(1, ROW), teacher.reshape(1, ROW), passages
    )
    begin = lax.axis_index("psg") * QD
    pair_loss = entropy + lax.dynamic_slice(total_terms, (0, begin), (1, QD))[0]
    return pair_loss, grad_queries.reshape(QD, QT, E), grad_passages


def solution(mesh):
    placed = (
        P(("psg", "qry"), None, None),
        P("psg", None, None),
        P(("psg", "qry"), None),
        P(("psg", "qry"), None),
    )
    return jax.shard_map(
        shards,
        mesh=mesh,
        in_specs=placed,
        out_specs=(P(("psg", "qry")), P(("psg", "qry"), None, None), P("psg", "qry", None)),
        check_vma=False,
    )
```

```python
import math

import jax
import jax.numpy as jnp
from jax import lax
from jax.experimental import pallas as pl
from jax.experimental.pallas import tpu as pltpu
from jax.sharding import PartitionSpec as P

MESH = pl.DeviceIdType.MESH
BF16, F32, I32 = jnp.bfloat16, jnp.float32, jnp.int32
HIGHEST = lax.Precision.HIGHEST
epsilon = 1e-06
softness_scale = 0.05

OWNERS, GROUPS, CHIPS = 32, 4, 16
QD, QT, C, E, PT, PS = 4, 32, 32, 128, 256, 32
CAP = 10
ROW = QD * QT
SHARE = PT // GROUPS
PER_CHUNK = 4
CHUNKS = (OWNERS * CAP + PS * (PER_CHUNK - 1)) // PER_CHUNK
UNROLL = 8
STEPS = CHUNKS // UNROLL
WIDE = 26
TERM_WIDE = 13
EARLY_TERMS = 4
SIDE = 4
OFFSETS = sorted(
    ((dy, dz) for dy in range(SIDE) for dz in range(SIDE) if dy or dz),
    key=lambda offset: sum(min(d, SIDE - d) for d in offset),
)
LINES = 128
PIECES = 4
PIECE = PS // 2 // PIECES
SLOTS = 512
LANES_PER_SENDER = SLOTS // OWNERS
ORDER = (2, 1, 3, 0)

NT = (((1,), (1,)), ((), ()))
TN = (((0,), (0,)), ((), ()))


def iota(shape, dim):
    return lax.broadcasted_iota(I32, shape, dim)


def dot(a, b, dims=None, precision=None):
    dims = (((1,), (0,)), ((), ())) if dims is None else dims
    return lax.dot_general(a, b, dims, precision=precision, preferred_element_type=F32)


def unit_of(values):
    inverse = lax.rsqrt(jnp.sum(values * values, -1, keepdims=True) + epsilon)
    return values * inverse, inverse


def project(values, gradient):
    unit, inverse = unit_of(values)
    return inverse * (gradient - unit * jnp.sum(unit * gradient, -1, keepdims=True))


def count(mask, axis):
    return jnp.sum(jnp.where(mask, 1, 0), axis, keepdims=True)


def as_row(block):
    return jnp.concatenate([block[index : index + 1] for index in range(block.shape[0])], 1)


def same(a, b):
    return (1 - jnp.minimum((a - b) * (a - b), 1)).astype(F32)


def column_of(row):
    return jnp.broadcast_to(row, (ROW, row.shape[1])).T[:, 0:1]


def slot_tables(ids, teacher):
    lane = iota((1, ROW), 1)
    ids, teacher = as_row(ids), as_row(teacher)
    power = jnp.exp(teacher)
    same_query = (iota((ROW, ROW), 0) // C == iota((ROW, ROW), 1) // C).astype(F32)
    power_sum = dot(jnp.broadcast_to(power, (8, ROW)), same_query, precision=HIGHEST)[0:1]
    target = power / power_sum
    owner = ids >> 5
    code = (lane >> 5) * PS + (ids & (PS - 1)) + 1
    ahead = iota((ROW, ROW), 0) < iota((ROW, ROW), 1)
    rank = count((column_of(owner) == owner) & ahead, 0)
    hits = owner == iota((OWNERS, ROW), 0)
    place = iota((OWNERS, ROW), 1) & (LANES_PER_SENDER - 1)
    codes = jnp.zeros((OWNERS, ROW), I32)
    targets = jnp.zeros((OWNERS, ROW), F32)
    for slot in range(CAP):
        chosen = hits & (rank == slot)
        codes = jnp.where(place == slot, jnp.sum(jnp.where(chosen, code, 0), 1, keepdims=True), codes)
        targets = jnp.where(place == slot, jnp.sum(jnp.where(chosen, target, 0.0), 1, keepdims=True), targets)
    entropy = target * (teacher - jnp.log(power_sum))
    return codes, targets, entropy


def order_slots(codes):
    lane = iota((OWNERS, SLOTS), 1)
    mine = lane >> 4 == iota((OWNERS, SLOTS), 0)
    code = jnp.sum(jnp.where(mine, jnp.concatenate([codes] * 4, 1), 0), 0, keepdims=True) - 1
    live = code >= 0
    local = code >> 5
    query = (iota((1, SLOTS), 1) >> 4) * QD + local
    passage = jnp.where(live, code & (PS - 1), -1)
    ahead = iota((SLOTS, SLOTS), 0) < iota((SLOTS, SLOTS), 1)
    rank = count((column_of(passage) == passage) & ahead, 0)
    index = iota((PS, SLOTS), 0)
    hits = passage == index
    chunks = (count(hits, 1) + (PER_CHUNK - 1)) >> 2
    chunk_row = jnp.sum(jnp.where(lane == index, chunks, 0), 0, keepdims=True)
    first = jnp.sum(jnp.where(lane < index, chunk_row, 0), 1, keepdims=True)
    place = rank + PER_CHUNK * jnp.sum(jnp.where(hits, first, 0), 0, keepdims=True)
    place = jnp.where(live, place, -1)
    ordered = column_of(place) == iota((SLOTS, SLOTS), 1)
    ordered = jnp.sum(jnp.where(ordered, column_of(query) + 1, 0), 0, keepdims=True) - 1
    inside = (first <= lane) & (lane < first + chunks)
    chunk_passage = jnp.sum(jnp.where(inside, index, 0), 0, keepdims=True)
    last = jnp.where(lane == index, jnp.maximum(first + chunks - 1, 0), 0)
    last = jnp.where(lane == index + ROW, jnp.minimum(chunks, 1), last)
    meta = [
        jnp.maximum(ordered, 0),
        chunk_passage,
        jnp.maximum(place, 0),
        jnp.where(live, 1, 0),
        jnp.sum(last, 0, keepdims=True),
    ]
    return meta, place, query


def place_values(place, query, targets):
    mine = iota((OWNERS, SLOTS), 1) >> 4 == iota((OWNERS, SLOTS), 0)
    target = jnp.sum(jnp.where(mine, jnp.concatenate([targets] * 4, 1), 0.0), 0, keepdims=True)
    segment = iota((LINES, ROW), 1) >> 5
    query_at = jnp.full((LINES, ROW), -1, I32)
    target_at = jnp.zeros((LINES, ROW), F32)
    for slot in range(PER_CHUNK):
        chosen = place == iota((LINES, SLOTS), 0) * PER_CHUNK + slot
        found = jnp.sum(jnp.where(chosen, query + 1, 0), 1, keepdims=True) - 1
        query_at = jnp.where(segment == slot, found, query_at)
        found = jnp.sum(jnp.where(chosen, target, 0.0), 1, keepdims=True)
        target_at = jnp.where(segment == slot, found, target_at)
    return query_at, target_at


def kernel(
    q_hbm, ids_hbm, teacher_hbm, passages_hbm,
    loss_out, gq_out, gp_out,
    q_ref, ids_ref, teacher_ref,
    q_all, raw, p_norm, p_turned, code_out, code_in, target_out, target_in, meta_v, meta_s, query_at, target_at, entropy,
    weights, terms, sides, totals_at, grads, own_grads, sums_out, sums_in, part_a, part_b, r2, r1, r3, r0,
    in_left, in_right, from_left, from_right, g_sib_out, g_sib_in, g_out, g_in,
    local_sem, q_send, q_recv, relay_send, relay_recv, code_send, code_recv, target_send, target_recv,
    sums_send, sums_recv, x_send, x_recv, sib_send, sib_recv, g_send, g_recv,
):
    me = lax.axis_index("psg")
    col = lax.axis_index("qry")
    chip, core = me // 2, me % 2
    sibling = chip * 2 + (1 - core)
    right, left = (col + 1) % GROUPS, (col + GROUPS - 1) % GROUPS

    y, z = chip // SIDE, chip % SIDE

    def chip_at(dy, dz):
        return ((y + dy) % SIDE) * SIDE + (z + dz) % SIDE

    far_first = [chip_at(dy, dz) for dy, dz in reversed(OFFSETS)]
    peers = [other * 2 + side for other in far_first for side in (core, 1 - core)] + [sibling]

    small = [
        pltpu.make_async_copy(q_hbm, q_ref, local_sem.at[5]),
        pltpu.make_async_copy(ids_hbm, ids_ref, local_sem.at[6]),
        pltpu.make_async_copy(teacher_hbm, teacher_ref, local_sem.at[7]),
    ]
    for load in small:
        load.start()

    barrier = pltpu.get_barrier_semaphore()
    for other in peers:
        pl.semaphore_signal(barrier, inc=1, device_id={"psg": other}, device_id_type=MESH)
    for side in (left, right):
        pl.semaphore_signal(barrier, inc=1, device_id={"qry": side}, device_id_type=MESH)

    loads = []
    for index, relative in enumerate(ORDER):
        share = (col + relative) % GROUPS
        load = pltpu.make_async_copy(
            passages_hbm.at[:, pl.ds(pl.multiple_of(share * SHARE, SHARE), SHARE), :],
            raw.at[:, pl.ds(index * SHARE, SHARE), :],
            local_sem.at[index],
        )
        load.start()
        loads.append(load)

    small[0].wait()
    q_raw = q_ref[...].astype(F32)
    own_rows = pl.ds(me * QD, QD)
    q_all[own_rows] = unit_of(q_raw)[0].astype(BF16).reshape(QD, QT, E)
    small[1].wait()
    small[2].wait()

    codes, targets, entropy[...] = slot_tables(ids_ref[...], teacher_ref[...])
    for owner in range(OWNERS):
        code_out[owner] = codes[owner : owner + 1]
        target_out[owner] = targets[owner : owner + 1]
    code_in[me] = code_out[me]
    target_in[me] = target_out[me]
    pl.semaphore_wait(barrier, OWNERS - 1 + 2)

    for other in peers:
        pltpu.make_async_remote_copy(
            src_ref=code_out.at[other], dst_ref=code_in.at[me], send_sem=code_send, recv_sem=code_recv,
            device_id={"psg": other}, device_id_type=MESH,
        ).start()

    def send_rows(rows, sender, dy, dz):
        pltpu.make_async_remote_copy(
            src_ref=q_all.at[rows], dst_ref=q_all.at[rows], send_sem=q_send, recv_sem=q_recv.at[sender],
            device_id={"psg": chip_at(dy, dz) * 2 + core}, device_id_type=MESH,
        ).start()

    def relay(rows):
        return pltpu.make_async_remote_copy(
            src_ref=q_all.at[rows], dst_ref=q_all.at[rows], send_sem=relay_send, recv_sem=relay_recv,
            device_id={"psg": sibling}, device_id_type=MESH,
        )

    ahead = 1 + 2 * core
    back = SIDE - ahead
    for dy, dz in (
        (ahead, 0), (0, ahead), (2, 2), (ahead, ahead), (ahead, back), (back, ahead), (back, 0), (0, back), (back, back)
    ):
        send_rows(own_rows, chip, dy, dz)
    relay(own_rows).start()

    for other in peers:
        pltpu.make_async_remote_copy(
            src_ref=target_out.at[other], dst_ref=target_in.at[me], send_sem=target_send, recv_sem=target_recv,
            device_id={"psg": other}, device_id_type=MESH,
        ).start()

    for load in loads:
        load.wait()

    def normalize(begin, end):
        def run(index, carry):
            values = raw[index].astype(F32)
            unit = unit_of(values)[0].astype(BF16)
            p_norm[index] = unit
            p_turned[index] = unit.T
            return carry

        lax.fori_loop(begin, end, run, 0, unroll=4)

    def hand_on(dy, dz, along_y=False, along_z=False):
        sender = chip_at(SIDE - dy, SIDE - dz)
        rows = pl.ds((sender * 2 + core) * QD, QD)
        pltpu.make_async_copy(q_all.at[rows], q_all.at[rows], q_recv.at[sender]).wait()
        if along_y:
            send_rows(rows, sender, ahead, 0)
        if along_z:
            send_rows(rows, sender, 0, ahead)
        relay(rows).start()

    normalize(0, 32)
    hand_on(ahead, 0, along_y=True)
    hand_on(0, ahead, along_z=True)
    hand_on(ahead, ahead, True, True)
    hand_on(ahead, back, along_y=True)
    hand_on(back, ahead, along_z=True)
    hand_on(back, 0)
    hand_on(0, back)
    hand_on(back, back)
    others = pl.ds(0, OWNERS - 1)
    pltpu.make_async_copy(code_in.at[others], code_in.at[others], code_recv).wait()
    meta, place, query_of = order_slots(jnp.concatenate([code_in[owner] for owner in range(OWNERS)], 0))
    for index, row in enumerate(meta):
        meta_v[index : index + 1, :] = row
    meta_v[5:8, :] = jnp.zeros((3, SLOTS), I32)
    hand_on(2, 0)
    hand_on(0, 2)
    to_scalar = pltpu.make_async_copy(meta_v, meta_s, local_sem.at[4])
    to_scalar.start()
    for dy, dz in ((2, ahead), (2, back), (ahead, 2), (back, 2), (2, 2)):
        hand_on(dy, dz)
    pltpu.make_async_copy(target_in.at[others], target_in.at[others], target_recv).wait()
    query_at[...], target_at[...] = place_values(
        place, query_of, jnp.concatenate([target_in[owner] for owner in range(OWNERS)], 0)
    )
    to_scalar.wait()
    half = pl.ds(0, CHIPS * QD)
    pltpu.make_async_copy(q_all.at[half], q_all.at[half], relay_recv).wait()

    factor = math.log2(math.e) / softness_scale

    def gather(chunk):
        return jnp.concatenate([q_all[meta_s[0, chunk * PER_CHUNK + slot]] for slot in range(PER_CHUNK)], 0)

    def forward(step, carry):
        for inner in range(WIDE):
            chunk = step * WIDE + inner
            tokens = p_norm[meta_s[1, chunk]]
            power = jnp.exp2(dot(tokens, gather(chunk), NT) * factor)
            weights[chunk] = power.astype(BF16)
            totals_at[chunk] = jnp.sum(power, 0, keepdims=True)
        return carry

    lax.fori_loop(0, CHUNKS // WIDE, forward, 0)
    lines = [totals_at[chunk] for chunk in range(CHUNKS)] + [jnp.ones((LINES - CHUNKS, ROW), F32)]
    logs = jnp.log(jnp.concatenate(lines, 0))

    lane = iota((LINES, ROW), 1)
    same_slot = (iota((ROW, ROW), 0) >> 5 == iota((ROW, ROW), 1) >> 5).astype(F32)
    score = dot(logs, same_slot, precision=HIGHEST) * softness_scale
    power = jnp.exp(score)
    target = target_at[...]
    shown = target * score
    power_sum = jnp.zeros((1, ROW), F32)
    shown_sum = jnp.zeros((1, ROW), F32)
    for slot in range(PER_CHUNK):
        pick = slice(slot * QT, slot * QT + 1)
        belongs = query_at[:, pick] == lane
        power_sum = power_sum + jnp.sum(jnp.where(belongs, power[:, pick], 0.0), 0, keepdims=True)
        shown_sum = shown_sum + jnp.sum(jnp.where(belongs, shown[:, pick], 0.0), 0, keepdims=True)
    sums_out[0:1, :] = power_sum
    sums_out[1:2, :] = shown_sum
    sums_in[me] = sums_out[...]

    for other in peers:
        pltpu.make_async_remote_copy(
            src_ref=sums_out, dst_ref=sums_in.at[me], send_sem=sums_send, recv_sem=sums_recv,
            device_id={"psg": other}, device_id_type=MESH,
        ).start()

    def scale(chunk, carry):
        inverse = 1.0 / totals_at[chunk]
        weights[chunk] = (weights[chunk].astype(F32) * inverse).astype(BF16)
        return carry

    lax.fori_loop(0, CHUNKS, scale, 0, unroll=13)

    unit = (iota((ROW, ROW), 0) == iota((ROW, ROW), 1)).astype(BF16)

    def query_term(step, carry):
        for inner in range(TERM_WIDE):
            chunk = step * TERM_WIDE + inner
            term = dot(p_turned[meta_s[1, chunk]], weights[chunk]).astype(BF16)
            term = dot(unit, term, NT).astype(BF16)
            terms[pl.ds(chunk * PER_CHUNK, PER_CHUNK)] = term.reshape(PER_CHUNK, QT, E)
        return carry

    lax.fori_loop(0, EARLY_TERMS, query_term, 0)

    pltpu.make_async_copy(sums_in.at[others], sums_in.at[others], sums_recv).wait()
    totals = sums_in[0]
    for owner in range(1, OWNERS):
        totals = totals + sums_in[owner]
    total_row = totals[0:1]
    slot_grads = []
    for slot in range(PER_CHUNK):
        pick = slice(slot * QT, slot * QT + 1)
        query = query_at[:, pick]
        total = jnp.sum(jnp.where(query == lane, total_row, 0.0), 1, keepdims=True)
        likelihood = power[:, pick] / jnp.where(query >= 0, total, 1.0)
        grad = jnp.where(query >= 0, likelihood - target[:, pick], 0.0)
        grads[slot] = jnp.broadcast_to(grad, (LINES, ROW))
        slot_grads.append((query & (QD - 1), grad))

    def passage_step(first, size, parts):
        def run(step, running):
            for inner in range(WIDE):
                chunk = step * WIDE + inner
                keep = same(meta_s[1, chunk], meta_s[1, jnp.maximum(chunk - 1, 0)])
                if first:
                    scale = [
                        jnp.broadcast_to(grads[slot, pl.ds(chunk, 1), :], (QT, E)) for slot in range(PER_CHUNK)
                    ]
                    side = (gather(chunk).astype(F32) * jnp.concatenate(scale, 0)).astype(BF16)
                    sides[chunk] = side
                    values = weights[chunk, 0:size]
                else:
                    side = sides[chunk]
                    values = weights[chunk, PT - size : PT]
                running = running * keep + dot(values, side)
                parts[chunk] = running.astype(BF16)
            return running

        lax.fori_loop(0, CHUNKS // WIDE, run, jnp.zeros((size, E), F32))

    def collect(parts, begin, out):
        def run(index, carry):
            used = meta_s[4, ROW + index].astype(F32)
            part = parts[meta_s[4, index]][begin : begin + SHARE].astype(F32) * used
            out[index] = part.astype(BF16)
            return carry

        lax.fori_loop(0, PS, run, 0, unroll=4)

    def send_piece(kind, piece, side, source, begin, target_ref, target_begin):
        index = kind * PIECES + piece
        copy = pltpu.make_async_remote_copy(
            src_ref=source.at[pl.ds(begin + piece * PIECE, PIECE)],
            dst_ref=target_ref.at[pl.ds(target_begin + piece * PIECE, PIECE)],
            send_sem=x_send.at[index],
            recv_sem=x_recv.at[index],
            device_id={"qry": side},
            device_id_type=MESH,
        )
        copy.start()
        return copy

    def send_pieces(kind, *rest):
        return [send_piece(kind, piece, *rest) for piece in range(PIECES)]

    passage_step(True, SHARE, part_a)
    collect(part_a, 0, r2)
    onward_right = send_pieces(0, right, r2, 0, in_left, 0)
    onward_left = send_pieces(1, left, r2, PS // 2, in_right, 0)
    passage_step(False, 3 * SHARE, part_b)
    collect(part_b, 0, r1)
    direct_right = send_pieces(2, right, r1, PS // 2, from_left, PS // 2)
    collect(part_b, SHARE, r3)
    direct_left = send_pieces(3, left, r3, 0, from_right, 0)
    collect(part_b, 2 * SHARE, r0)

    def query_block(sender):
        sums = [jnp.zeros((QT, E), F32) for _ in range(QD)]
        for slot in range(CAP):
            place = meta_s[2, sender * LANES_PER_SENDER + slot]
            live = meta_s[3, sender * LANES_PER_SENDER + slot].astype(F32)
            term = terms[place].astype(F32) * live
            for query in range(QD):
                sums[query] = sums[query] + term * own_grads[query, place & 3, pl.ds(place >> 2, 1), :]
        return jnp.concatenate(sums, 0)

    def for_sibling(index, carry):
        g_sib_out[index] = query_block(index * 2 + (1 - core)).astype(BF16)
        return carry

    def for_chips(index, carry):
        g_out[index] = query_block(index * 2 + core).astype(BF16)
        return carry

    loss_row = jnp.log(total_row) - totals[1:2]
    one_lane = iota((1, ROW), 1)
    loss = jnp.zeros((1, ROW), F32)
    for query in range(QD):
        mine = jnp.sum(jnp.where(one_lane == me * QD + query, loss_row, 0.0), 1, keepdims=True)
        mine = mine + jnp.sum(jnp.where(one_lane >> 5 == query, entropy[...], 0.0), 1, keepdims=True)
        loss = jnp.where(one_lane == query, mine, loss)
    loss_out[...] = loss
    lax.fori_loop(EARLY_TERMS, CHUNKS // TERM_WIDE, query_term, 0)
    for slot, (local, grad) in enumerate(slot_grads):
        for query in range(QD):
            mine = jnp.where(local == query, grad, 0.0)
            own_grads[query, slot] = jnp.broadcast_to(mine, (LINES, ROW))

    lax.fori_loop(0, CHIPS, for_sibling, 0)
    to_sibling = pltpu.make_async_remote_copy(
        src_ref=g_sib_out, dst_ref=g_sib_in, send_sem=sib_send, recv_sem=sib_recv,
        device_id={"psg": sibling}, device_id_type=MESH,
    )
    to_sibling.start()
    lax.fori_loop(0, CHIPS, for_chips, 0)
    to_sibling.wait_recv()

    def add_sibling(index, carry):
        g_out[index] = (g_out[index].astype(F32) + g_sib_in[index].astype(F32)).astype(BF16)
        return carry

    lax.fori_loop(0, CHIPS, add_sibling, 0)

    for other in far_first:
        pltpu.make_async_remote_copy(
            src_ref=g_out.at[other], dst_ref=g_in.at[chip], send_sem=g_send, recv_sem=g_recv,
            device_id={"psg": other * 2 + core}, device_id_type=MESH,
        ).start()
    g_in[chip] = g_out[chip]

    def merge(incoming, out, begin, piece):
        for index in range(piece * PIECE, (piece + 1) * PIECE):
            both = out[begin + index].astype(F32) + incoming[index].astype(F32)
            out[begin + index] = both.astype(BF16)

    final_right, final_left = [], []
    for piece in range(PIECES):
        onward_right[piece].wait_recv()
        merge(in_left, r1, 0, piece)
        onward_left[piece].wait_recv()
        merge(in_right, r3, PS // 2, piece)
        final_right.append(send_piece(4, piece, right, r1, 0, from_left, 0))
        final_left.append(send_piece(5, piece, left, r3, PS // 2, from_right, PS // 2))

    fewer = pl.ds(0, CHIPS - 1)
    pltpu.make_async_copy(g_in.at[fewer], g_in.at[fewer], g_recv).wait()
    gradient = jnp.zeros((ROW, E), F32)
    for index in range(CHIPS):
        gradient = gradient + g_in[index].astype(F32)
    gq_out[...] = project(q_ref[...].astype(F32), gradient).astype(BF16)

    def finish(index):
        gradient = r0[index].astype(F32) + from_left[index].astype(F32) + from_right[index].astype(F32)
        values = raw[index, 3 * SHARE : 4 * SHARE, :].astype(F32)
        gp_out[index] = project(values, gradient).astype(BF16)

    for copy in (*direct_right, *direct_left):
        copy.wait_recv()
    for piece in range(PIECES):
        final_right[piece].wait_recv()
        final_left[piece].wait_recv()
        for base in (piece * PIECE, PS // 2 + piece * PIECE):
            for inner in range(PIECE):
                finish(base + inner)

    for copy in (*onward_right, *onward_left, *direct_right, *direct_left, *final_right, *final_left, to_sibling):
        copy.wait_send()
    pltpu.make_async_copy(code_in.at[others], code_in.at[others], code_send).wait()
    pltpu.make_async_copy(target_in.at[others], target_in.at[others], target_send).wait()
    pltpu.make_async_copy(sums_in.at[others], sums_in.at[others], sums_send).wait()
    pltpu.make_async_copy(g_in.at[fewer], g_in.at[fewer], g_send).wait()
    sent = pl.ds(0, (CHIPS - 1) * QD)
    pltpu.make_async_copy(q_all.at[sent], q_all.at[sent], q_send).wait()
    pltpu.make_async_copy(q_all.at[half], q_all.at[half], relay_send).wait()


def deliver(loss_in, gq_in, gp_in, loss_out, gq_out, gp_out):
    loss_out[...] = loss_in[:, 0:QD]
    gq_out[...] = gq_in[...]
    gp_out[...] = gp_in[...]


def step(queries, ids, teacher, passages):
    dma = pltpu.SemaphoreType.DMA
    vmem = pltpu.VMEM
    share = (PS, SHARE, E)
    half_share = (PS // 2, SHARE, E)
    owner_block = (CHIPS, ROW, E)
    return pl.pallas_call(
        kernel,
        out_shape=(
            jax.ShapeDtypeStruct((1, ROW), F32),
            jax.ShapeDtypeStruct((ROW, E), BF16),
            jax.ShapeDtypeStruct(share, BF16),
        ),
        in_specs=[pl.BlockSpec(memory_space=pltpu.HBM)] * 4,
        out_specs=(pl.BlockSpec(memory_space=pltpu.VMEM),) * 3,
        scratch_shapes=[
            vmem((ROW, E), BF16),
            vmem((QD, C), I32),
            vmem((QD, C), F32),
            vmem((OWNERS * QD, QT, E), BF16),
            vmem((PS, PT, E), BF16),
            vmem((PS, PT, E), BF16),
            vmem((PS, E, PT), BF16),
            vmem((OWNERS, 1, ROW), I32),
            vmem((OWNERS, 1, ROW), I32),
            vmem((OWNERS, 1, ROW), F32),
            vmem((OWNERS, 1, ROW), F32),
            vmem((8, SLOTS), I32),
            pltpu.SMEM((8, SLOTS), I32),
            vmem((LINES, ROW), I32),
            vmem((LINES, ROW), F32),
            vmem((1, ROW), F32),
            vmem((CHUNKS, PT, ROW), BF16),
            vmem((CHUNKS * PER_CHUNK, QT, E), BF16),
            vmem((CHUNKS, ROW, E), BF16),
            vmem((CHUNKS, 1, ROW), F32),
            vmem((PER_CHUNK, LINES, ROW), F32),
            vmem((QD, PER_CHUNK, LINES, ROW), F32),
            vmem((2, ROW), F32),
            vmem((OWNERS, 2, ROW), F32),
            vmem((CHUNKS, SHARE, E), BF16),
            vmem((CHUNKS, 3 * SHARE, E), BF16),
            vmem(share, BF16),
            vmem(share, BF16),
            vmem(share, BF16),
            vmem(share, BF16),
            vmem(half_share, BF16),
            vmem(half_share, BF16),
            vmem(share, BF16),
            vmem(share, BF16),
            vmem(owner_block, BF16),
            vmem(owner_block, BF16),
            vmem(owner_block, BF16),
            vmem(owner_block, BF16),
            dma((8,)),
            dma,
            dma((CHIPS,)),
            dma,
            dma,
            dma,
            dma,
            dma,
            dma,
            dma,
            dma,
            dma((6 * PIECES,)),
            dma((6 * PIECES,)),
            dma,
            dma,
            dma,
            dma,
        ],
        compiler_params=pltpu.CompilerParams(collective_id=0, has_side_effects=True, vmem_limit_bytes=44 << 20),
    )(*(pltpu.with_memory_space_constraint(value, pltpu.HBM) for value in (queries, ids, teacher, passages)))


def shards(queries, passages, candidates, teacher):
    loss, grad_queries, grad_passages = step(queries.reshape(ROW, E), candidates, teacher, passages)
    loss, grad_queries, grad_passages = pl.pallas_call(
        deliver,
        out_shape=(
            jax.ShapeDtypeStruct((1, QD), F32),
            jax.ShapeDtypeStruct(grad_queries.shape, BF16),
            jax.ShapeDtypeStruct(grad_passages.shape, BF16),
        ),
        in_specs=[pl.BlockSpec(memory_space=pltpu.VMEM)] * 3,
        out_specs=(pl.BlockSpec(memory_space=pltpu.VMEM),) * 3,
        compiler_params=pltpu.CompilerParams(vmem_limit_bytes=4 << 20),
    )(loss, grad_queries, grad_passages)
    return loss.reshape(QD), grad_queries.reshape(QD, QT, E), grad_passages


def solution(mesh):
    placed = (
        P(("psg", "qry"), None, None),
        P("psg", None, None),
        P(("psg", "qry"), None),
        P(("psg", "qry"), None),
    )
    return jax.shard_map(
        shards,
        mesh=mesh,
        in_specs=placed,
        out_specs=(P(("psg", "qry")), P(("psg", "qry"), None, None), P("psg", "qry", None)),
        check_vma=False,
    )
```

```python
import math

import jax
import jax.numpy as jnp
from jax import lax
from jax.experimental import pallas as pl
from jax.experimental.pallas import tpu as pltpu
from jax.sharding import PartitionSpec as P

MESH = pl.DeviceIdType.MESH
BF16, F32, I32 = jnp.bfloat16, jnp.float32, jnp.int32
HIGHEST = lax.Precision.HIGHEST
epsilon = 1e-06
softness_scale = 0.05

OWNERS, GROUPS, CHIPS = 32, 4, 16
QD, QT, C, E, PT, PS = 4, 32, 32, 128, 256, 32
CAP = 10
ROW = QD * QT
SHARE = PT // GROUPS
PER_CHUNK = 4
CHUNKS = (OWNERS * CAP + PS * (PER_CHUNK - 1)) // PER_CHUNK
UNROLL = 8
STEPS = CHUNKS // UNROLL
WIDE = 26
TERM_WIDE = 13
EARLY_TERMS = 3
SIDE = 4
OFFSETS = sorted(
    ((dy, dz) for dy in range(SIDE) for dz in range(SIDE) if dy or dz),
    key=lambda offset: sum(min(d, SIDE - d) for d in offset),
)
LINES = 128
PIECES = 4
PIECE = PS // 2 // PIECES
SLOTS = 512
LANES_PER_SENDER = SLOTS // OWNERS
ORDER = (2, 1, 3, 0)

NT = (((1,), (1,)), ((), ()))
TN = (((0,), (0,)), ((), ()))


def iota(shape, dim):
    return lax.broadcasted_iota(I32, shape, dim)


def dot(a, b, dims=None, precision=None):
    dims = (((1,), (0,)), ((), ())) if dims is None else dims
    return lax.dot_general(a, b, dims, precision=precision, preferred_element_type=F32)


def unit_of(values):
    inverse = lax.rsqrt(jnp.sum(values * values, -1, keepdims=True) + epsilon)
    return values * inverse, inverse


def project(values, gradient):
    unit, inverse = unit_of(values)
    return inverse * (gradient - unit * jnp.sum(unit * gradient, -1, keepdims=True))


def count(mask, axis):
    return jnp.sum(jnp.where(mask, 1, 0), axis, keepdims=True)


def as_row(block):
    return jnp.concatenate([block[index : index + 1] for index in range(block.shape[0])], 1)


def same(a, b):
    return (1 - jnp.minimum((a - b) * (a - b), 1)).astype(F32)


def column_of(row):
    return jnp.broadcast_to(row, (ROW, row.shape[1])).T[:, 0:1]


def slot_tables(ids, teacher):
    lane = iota((1, ROW), 1)
    ids, teacher = as_row(ids), as_row(teacher)
    power = jnp.exp(teacher)
    same_query = (iota((ROW, ROW), 0) // C == iota((ROW, ROW), 1) // C).astype(F32)
    power_sum = dot(jnp.broadcast_to(power, (8, ROW)), same_query, precision=HIGHEST)[0:1]
    target = power / power_sum
    owner = ids >> 5
    code = (lane >> 5) * PS + (ids & (PS - 1)) + 1
    ahead = iota((ROW, ROW), 0) < iota((ROW, ROW), 1)
    rank = count((column_of(owner) == owner) & ahead, 0)
    hits = owner == iota((OWNERS, ROW), 0)
    place = iota((OWNERS, ROW), 1) & (LANES_PER_SENDER - 1)
    codes = jnp.zeros((OWNERS, ROW), I32)
    targets = jnp.zeros((OWNERS, ROW), F32)
    for slot in range(CAP):
        chosen = hits & (rank == slot)
        codes = jnp.where(place == slot, jnp.sum(jnp.where(chosen, code, 0), 1, keepdims=True), codes)
        targets = jnp.where(place == slot, jnp.sum(jnp.where(chosen, target, 0.0), 1, keepdims=True), targets)
    entropy = target * (teacher - jnp.log(power_sum))
    return codes, targets, entropy


def order_slots(codes):
    lane = iota((OWNERS, SLOTS), 1)
    mine = lane >> 4 == iota((OWNERS, SLOTS), 0)
    code = jnp.sum(jnp.where(mine, jnp.concatenate([codes] * 4, 1), 0), 0, keepdims=True) - 1
    live = code >= 0
    local = code >> 5
    query = (iota((1, SLOTS), 1) >> 4) * QD + local
    passage = jnp.where(live, code & (PS - 1), -1)
    ahead = iota((SLOTS, SLOTS), 0) < iota((SLOTS, SLOTS), 1)
    rank = count((column_of(passage) == passage) & ahead, 0)
    index = iota((PS, SLOTS), 0)
    hits = passage == index
    chunks = (count(hits, 1) + (PER_CHUNK - 1)) >> 2
    chunk_row = jnp.sum(jnp.where(lane == index, chunks, 0), 0, keepdims=True)
    first = jnp.sum(jnp.where(lane < index, chunk_row, 0), 1, keepdims=True)
    place = rank + PER_CHUNK * jnp.sum(jnp.where(hits, first, 0), 0, keepdims=True)
    place = jnp.where(live, place, -1)
    ordered = column_of(place) == iota((SLOTS, SLOTS), 1)
    ordered = jnp.sum(jnp.where(ordered, column_of(query) + 1, 0), 0, keepdims=True) - 1
    inside = (first <= lane) & (lane < first + chunks)
    chunk_passage = jnp.sum(jnp.where(inside, index, 0), 0, keepdims=True)
    last = jnp.where(lane == index, jnp.maximum(first + chunks - 1, 0), 0)
    last = jnp.where(lane == index + ROW, jnp.minimum(chunks, 1), last)
    meta = [
        jnp.maximum(ordered, 0),
        chunk_passage,
        jnp.maximum(place, 0),
        jnp.where(live, 1, 0),
        jnp.sum(last, 0, keepdims=True),
    ]
    return meta, place, query


def place_values(place, query, targets):
    mine = iota((OWNERS, SLOTS), 1) >> 4 == iota((OWNERS, SLOTS), 0)
    target = jnp.sum(jnp.where(mine, jnp.concatenate([targets] * 4, 1), 0.0), 0, keepdims=True)
    segment = iota((LINES, ROW), 1) >> 5
    query_at = jnp.full((LINES, ROW), -1, I32)
    target_at = jnp.zeros((LINES, ROW), F32)
    for slot in range(PER_CHUNK):
        chosen = place == iota((LINES, SLOTS), 0) * PER_CHUNK + slot
        found = jnp.sum(jnp.where(chosen, query + 1, 0), 1, keepdims=True) - 1
        query_at = jnp.where(segment == slot, found, query_at)
        found = jnp.sum(jnp.where(chosen, target, 0.0), 1, keepdims=True)
        target_at = jnp.where(segment == slot, found, target_at)
    return query_at, target_at


def kernel(
    q_hbm, ids_hbm, teacher_hbm, passages_hbm,
    loss_out, gq_out, gp_out,
    q_ref, ids_ref, teacher_ref,
    q_all, raw, p_norm, p_turned, code_out, code_in, target_out, target_in, meta_v, meta_s, query_at, target_at, entropy,
    weights, terms, sides, totals_at, grads, own_grads, sums_out, sums_in, part_a, part_b, r2, r1, r3, r0,
    in_left, in_right, from_left, from_right, g_sib_out, g_sib_in, g_out, g_in,
    local_sem, q_send, q_recv, relay_send, relay_recv, code_send, code_recv, target_send, target_recv,
    sums_send, sums_recv, x_send, x_recv, sib_send, sib_recv, g_send, g_recv,
):
    me = lax.axis_index("psg")
    col = lax.axis_index("qry")
    chip, core = me // 2, me % 2
    sibling = chip * 2 + (1 - core)
    right, left = (col + 1) % GROUPS, (col + GROUPS - 1) % GROUPS

    y, z = chip // SIDE, chip % SIDE

    def chip_at(dy, dz):
        return ((y + dy) % SIDE) * SIDE + (z + dz) % SIDE

    far_first = [chip_at(dy, dz) for dy, dz in reversed(OFFSETS)]
    peers = [other * 2 + side for other in far_first for side in (core, 1 - core)] + [sibling]

    small = [
        pltpu.make_async_copy(q_hbm, q_ref, local_sem.at[5]),
        pltpu.make_async_copy(ids_hbm, ids_ref, local_sem.at[6]),
        pltpu.make_async_copy(teacher_hbm, teacher_ref, local_sem.at[7]),
    ]
    for load in small:
        load.start()

    barrier = pltpu.get_barrier_semaphore()
    for other in peers:
        pl.semaphore_signal(barrier, inc=1, device_id={"psg": other}, device_id_type=MESH)
    for side in (left, right):
        pl.semaphore_signal(barrier, inc=1, device_id={"qry": side}, device_id_type=MESH)

    loads = []
    for index, relative in enumerate(ORDER):
        share = (col + relative) % GROUPS
        load = pltpu.make_async_copy(
            passages_hbm.at[:, pl.ds(pl.multiple_of(share * SHARE, SHARE), SHARE), :],
            raw.at[:, pl.ds(index * SHARE, SHARE), :],
            local_sem.at[index],
        )
        load.start()
        loads.append(load)

    small[0].wait()
    q_raw = q_ref[...].astype(F32)
    own_rows = pl.ds(me * QD, QD)
    q_all[own_rows] = unit_of(q_raw)[0].astype(BF16).reshape(QD, QT, E)
    small[1].wait()
    small[2].wait()

    codes, targets, entropy[...] = slot_tables(ids_ref[...], teacher_ref[...])
    for owner in range(OWNERS):
        code_out[owner] = codes[owner : owner + 1]
        target_out[owner] = targets[owner : owner + 1]
    code_in[me] = code_out[me]
    target_in[me] = target_out[me]
    pl.semaphore_wait(barrier, OWNERS - 1 + 2)

    for other in peers:
        pltpu.make_async_remote_copy(
            src_ref=code_out.at[other], dst_ref=code_in.at[me], send_sem=code_send, recv_sem=code_recv,
            device_id={"psg": other}, device_id_type=MESH,
        ).start()

    def send_rows(rows, sender, dy, dz):
        pltpu.make_async_remote_copy(
            src_ref=q_all.at[rows], dst_ref=q_all.at[rows], send_sem=q_send, recv_sem=q_recv.at[sender],
            device_id={"psg": chip_at(dy, dz) * 2 + core}, device_id_type=MESH,
        ).start()

    def relay(rows):
        return pltpu.make_async_remote_copy(
            src_ref=q_all.at[rows], dst_ref=q_all.at[rows], send_sem=relay_send, recv_sem=relay_recv,
            device_id={"psg": sibling}, device_id_type=MESH,
        )

    ahead = 1 + 2 * core
    back = SIDE - ahead
    for dy, dz in (
        (ahead, 0), (0, ahead), (2, 2), (ahead, ahead), (ahead, back), (back, ahead), (back, 0), (0, back), (back, back)
    ):
        send_rows(own_rows, chip, dy, dz)
    relay(own_rows).start()

    for other in peers:
        pltpu.make_async_remote_copy(
            src_ref=target_out.at[other], dst_ref=target_in.at[me], send_sem=target_send, recv_sem=target_recv,
            device_id={"psg": other}, device_id_type=MESH,
        ).start()

    for load in loads:
        load.wait()

    def normalize(begin, end):
        def run(index, carry):
            values = raw[index].astype(F32)
            unit = unit_of(values)[0].astype(BF16)
            p_norm[index] = unit
            p_turned[index] = unit.T
            return carry

        lax.fori_loop(begin, end, run, 0, unroll=4)

    def hand_on(dy, dz, along_y=False, along_z=False):
        sender = chip_at(SIDE - dy, SIDE - dz)
        rows = pl.ds((sender * 2 + core) * QD, QD)
        pltpu.make_async_copy(q_all.at[rows], q_all.at[rows], q_recv.at[sender]).wait()
        if along_y:
            send_rows(rows, sender, ahead, 0)
        if along_z:
            send_rows(rows, sender, 0, ahead)
        relay(rows).start()

    normalize(0, 32)
    hand_on(ahead, 0, along_y=True)
    hand_on(0, ahead, along_z=True)
    hand_on(ahead, ahead, True, True)
    hand_on(ahead, back, along_y=True)
    hand_on(back, ahead, along_z=True)
    hand_on(back, 0)
    hand_on(0, back)
    hand_on(back, back)
    others = pl.ds(0, OWNERS - 1)
    pltpu.make_async_copy(code_in.at[others], code_in.at[others], code_recv).wait()
    meta, place, query_of = order_slots(jnp.concatenate([code_in[owner] for owner in range(OWNERS)], 0))
    for index, row in enumerate(meta):
        meta_v[index : index + 1, :] = row
    meta_v[5:8, :] = jnp.zeros((3, SLOTS), I32)
    hand_on(2, 0)
    hand_on(0, 2)
    to_scalar = pltpu.make_async_copy(meta_v, meta_s, local_sem.at[4])
    to_scalar.start()
    for dy, dz in ((2, ahead), (2, back), (ahead, 2), (back, 2), (2, 2)):
        hand_on(dy, dz)
    pltpu.make_async_copy(target_in.at[others], target_in.at[others], target_recv).wait()
    query_at[...], target_at[...] = place_values(
        place, query_of, jnp.concatenate([target_in[owner] for owner in range(OWNERS)], 0)
    )
    to_scalar.wait()
    half = pl.ds(0, CHIPS * QD)
    pltpu.make_async_copy(q_all.at[half], q_all.at[half], relay_recv).wait()

    factor = math.log2(math.e) / softness_scale

    def gather(chunk):
        return jnp.concatenate([q_all[meta_s[0, chunk * PER_CHUNK + slot]] for slot in range(PER_CHUNK)], 0)

    def forward(step, carry):
        for inner in range(WIDE):
            chunk = step * WIDE + inner
            tokens = p_norm[meta_s[1, chunk]]
            power = jnp.exp2(dot(tokens, gather(chunk), NT) * factor)
            weights[chunk] = power.astype(BF16)
            totals_at[chunk] = jnp.sum(power, 0, keepdims=True)
        return carry

    lax.fori_loop(0, CHUNKS // WIDE, forward, 0)
    lines = [totals_at[chunk] for chunk in range(CHUNKS)] + [jnp.ones((LINES - CHUNKS, ROW), F32)]
    logs = jnp.log(jnp.concatenate(lines, 0))

    lane = iota((LINES, ROW), 1)
    same_slot = (iota((ROW, ROW), 0) >> 5 == iota((ROW, ROW), 1) >> 5).astype(F32)
    score = dot(logs, same_slot, precision=HIGHEST) * softness_scale
    power = jnp.exp(score)
    target = target_at[...]
    shown = target * score
    power_sum = jnp.zeros((1, ROW), F32)
    shown_sum = jnp.zeros((1, ROW), F32)
    for slot in range(PER_CHUNK):
        pick = slice(slot * QT, slot * QT + 1)
        belongs = query_at[:, pick] == lane
        power_sum = power_sum + jnp.sum(jnp.where(belongs, power[:, pick], 0.0), 0, keepdims=True)
        shown_sum = shown_sum + jnp.sum(jnp.where(belongs, shown[:, pick], 0.0), 0, keepdims=True)
    sums_out[0:1, :] = power_sum
    sums_out[1:2, :] = shown_sum
    sums_in[me] = sums_out[...]

    for other in peers:
        pltpu.make_async_remote_copy(
            src_ref=sums_out, dst_ref=sums_in.at[me], send_sem=sums_send, recv_sem=sums_recv,
            device_id={"psg": other}, device_id_type=MESH,
        ).start()

    def scale(chunk, carry):
        inverse = 1.0 / totals_at[chunk]
        weights[chunk] = (weights[chunk].astype(F32) * inverse).astype(BF16)
        return carry

    lax.fori_loop(0, CHUNKS, scale, 0, unroll=13)

    def query_term(step, carry):
        for inner in range(TERM_WIDE):
            chunk = step * TERM_WIDE + inner
            term = dot(p_turned[meta_s[1, chunk]], weights[chunk]).astype(BF16)
            terms[pl.ds(chunk * PER_CHUNK, PER_CHUNK)] = term.T.reshape(PER_CHUNK, QT, E)
        return carry

    lax.fori_loop(0, EARLY_TERMS, query_term, 0)

    pltpu.make_async_copy(sums_in.at[others], sums_in.at[others], sums_recv).wait()
    totals = sums_in[0]
    for owner in range(1, OWNERS):
        totals = totals + sums_in[owner]
    total_row = totals[0:1]
    slot_grads = []
    for slot in range(PER_CHUNK):
        pick = slice(slot * QT, slot * QT + 1)
        query = query_at[:, pick]
        total = jnp.sum(jnp.where(query == lane, total_row, 0.0), 1, keepdims=True)
        likelihood = power[:, pick] / jnp.where(query >= 0, total, 1.0)
        grad = jnp.where(query >= 0, likelihood - target[:, pick], 0.0)
        grads[slot] = jnp.broadcast_to(grad, (LINES, ROW))
        slot_grads.append((query & (QD - 1), grad))

    def passage_step(first, size, parts):
        def run(step, running):
            for inner in range(WIDE):
                chunk = step * WIDE + inner
                keep = same(meta_s[1, chunk], meta_s[1, jnp.maximum(chunk - 1, 0)])
                if first:
                    scale = [
                        jnp.broadcast_to(grads[slot, pl.ds(chunk, 1), :], (QT, E)) for slot in range(PER_CHUNK)
                    ]
                    side = (gather(chunk).astype(F32) * jnp.concatenate(scale, 0)).astype(BF16)
                    sides[chunk] = side
                    values = weights[chunk, 0:size]
                else:
                    side = sides[chunk]
                    values = weights[chunk, PT - size : PT]
                running = running * keep + dot(values, side)
                parts[chunk] = running.astype(BF16)
            return running

        lax.fori_loop(0, CHUNKS // WIDE, run, jnp.zeros((size, E), F32))

    def collect(parts, begin, out):
        def run(index, carry):
            used = meta_s[4, ROW + index].astype(F32)
            part = parts[meta_s[4, index]][begin : begin + SHARE].astype(F32) * used
            out[index] = part.astype(BF16)
            return carry

        lax.fori_loop(0, PS, run, 0, unroll=4)

    def send_piece(kind, piece, side, source, begin, target_ref, target_begin):
        index = kind * PIECES + piece
        copy = pltpu.make_async_remote_copy(
            src_ref=source.at[pl.ds(begin + piece * PIECE, PIECE)],
            dst_ref=target_ref.at[pl.ds(target_begin + piece * PIECE, PIECE)],
            send_sem=x_send.at[index],
            recv_sem=x_recv.at[index],
            device_id={"qry": side},
            device_id_type=MESH,
        )
        copy.start()
        return copy

    def send_pieces(kind, *rest):
        return [send_piece(kind, piece, *rest) for piece in range(PIECES)]

    passage_step(True, SHARE, part_a)
    collect(part_a, 0, r2)
    onward_right = send_pieces(0, right, r2, 0, in_left, 0)
    onward_left = send_pieces(1, left, r2, PS // 2, in_right, 0)
    passage_step(False, 3 * SHARE, part_b)
    collect(part_b, 0, r1)
    direct_right = send_pieces(2, right, r1, PS // 2, from_left, PS // 2)
    collect(part_b, SHARE, r3)
    direct_left = send_pieces(3, left, r3, 0, from_right, 0)
    collect(part_b, 2 * SHARE, r0)

    def query_block(sender):
        sums = [jnp.zeros((QT, E), F32) for _ in range(QD)]
        for slot in range(CAP):
            place = meta_s[2, sender * LANES_PER_SENDER + slot]
            live = meta_s[3, sender * LANES_PER_SENDER + slot].astype(F32)
            term = terms[place].astype(F32) * live
            for query in range(QD):
                sums[query] = sums[query] + term * own_grads[query, place & 3, pl.ds(place >> 2, 1), :]
        return jnp.concatenate(sums, 0)

    def for_sibling(index, carry):
        g_sib_out[index] = query_block(index * 2 + (1 - core)).astype(BF16)
        return carry

    def for_chips(index, carry):
        g_out[index] = query_block(index * 2 + core).astype(BF16)
        return carry

    loss_row = jnp.log(total_row) - totals[1:2]
    one_lane = iota((1, ROW), 1)
    loss = jnp.zeros((1, ROW), F32)
    for query in range(QD):
        mine = jnp.sum(jnp.where(one_lane == me * QD + query, loss_row, 0.0), 1, keepdims=True)
        mine = mine + jnp.sum(jnp.where(one_lane >> 5 == query, entropy[...], 0.0), 1, keepdims=True)
        loss = jnp.where(one_lane == query, mine, loss)
    loss_out[...] = loss
    lax.fori_loop(EARLY_TERMS, CHUNKS // TERM_WIDE, query_term, 0)
    for slot, (local, grad) in enumerate(slot_grads):
        for query in range(QD):
            mine = jnp.where(local == query, grad, 0.0)
            own_grads[query, slot] = jnp.broadcast_to(mine, (LINES, ROW))

    lax.fori_loop(0, CHIPS, for_sibling, 0)
    to_sibling = pltpu.make_async_remote_copy(
        src_ref=g_sib_out, dst_ref=g_sib_in, send_sem=sib_send, recv_sem=sib_recv,
        device_id={"psg": sibling}, device_id_type=MESH,
    )
    to_sibling.start()
    lax.fori_loop(0, CHIPS, for_chips, 0)
    to_sibling.wait_recv()

    def add_sibling(index, carry):
        g_out[index] = (g_out[index].astype(F32) + g_sib_in[index].astype(F32)).astype(BF16)
        return carry

    lax.fori_loop(0, CHIPS, add_sibling, 0)

    for other in far_first:
        pltpu.make_async_remote_copy(
            src_ref=g_out.at[other], dst_ref=g_in.at[chip], send_sem=g_send, recv_sem=g_recv,
            device_id={"psg": other * 2 + core}, device_id_type=MESH,
        ).start()
    g_in[chip] = g_out[chip]

    def merge(incoming, out, begin, piece):
        for index in range(piece * PIECE, (piece + 1) * PIECE):
            both = out[begin + index].astype(F32) + incoming[index].astype(F32)
            out[begin + index] = both.astype(BF16)

    final_right, final_left = [], []
    for piece in range(PIECES):
        onward_right[piece].wait_recv()
        merge(in_left, r1, 0, piece)
        onward_left[piece].wait_recv()
        merge(in_right, r3, PS // 2, piece)
        final_right.append(send_piece(4, piece, right, r1, 0, from_left, 0))
        final_left.append(send_piece(5, piece, left, r3, PS // 2, from_right, PS // 2))

    fewer = pl.ds(0, CHIPS - 1)
    pltpu.make_async_copy(g_in.at[fewer], g_in.at[fewer], g_recv).wait()
    gradient = jnp.zeros((ROW, E), F32)
    for index in range(CHIPS):
        gradient = gradient + g_in[index].astype(F32)
    gq_out[...] = project(q_ref[...].astype(F32), gradient).astype(BF16)

    def finish(index):
        gradient = r0[index].astype(F32) + from_left[index].astype(F32) + from_right[index].astype(F32)
        values = raw[index, 3 * SHARE : 4 * SHARE, :].astype(F32)
        gp_out[index] = project(values, gradient).astype(BF16)

    for copy in (*direct_right, *direct_left):
        copy.wait_recv()
    for piece in range(PIECES):
        final_right[piece].wait_recv()
        final_left[piece].wait_recv()
        for base in (piece * PIECE, PS // 2 + piece * PIECE):
            for inner in range(PIECE):
                finish(base + inner)

    for copy in (*onward_right, *onward_left, *direct_right, *direct_left, *final_right, *final_left, to_sibling):
        copy.wait_send()
    pltpu.make_async_copy(code_in.at[others], code_in.at[others], code_send).wait()
    pltpu.make_async_copy(target_in.at[others], target_in.at[others], target_send).wait()
    pltpu.make_async_copy(sums_in.at[others], sums_in.at[others], sums_send).wait()
    pltpu.make_async_copy(g_in.at[fewer], g_in.at[fewer], g_send).wait()
    sent = pl.ds(0, (CHIPS - 1) * QD)
    pltpu.make_async_copy(q_all.at[sent], q_all.at[sent], q_send).wait()
    pltpu.make_async_copy(q_all.at[half], q_all.at[half], relay_send).wait()


def deliver(loss_in, gq_in, gp_in, loss_out, gq_out, gp_out):
    loss_out[...] = loss_in[:, 0:QD]
    gq_out[...] = gq_in[...]
    gp_out[...] = gp_in[...]


def step(queries, ids, teacher, passages):
    dma = pltpu.SemaphoreType.DMA
    vmem = pltpu.VMEM
    share = (PS, SHARE, E)
    half_share = (PS // 2, SHARE, E)
    owner_block = (CHIPS, ROW, E)
    return pl.pallas_call(
        kernel,
        out_shape=(
            jax.ShapeDtypeStruct((1, ROW), F32),
            jax.ShapeDtypeStruct((ROW, E), BF16),
            jax.ShapeDtypeStruct(share, BF16),
        ),
        in_specs=[pl.BlockSpec(memory_space=pltpu.HBM)] * 4,
        out_specs=(pl.BlockSpec(memory_space=pltpu.VMEM),) * 3,
        scratch_shapes=[
            vmem((ROW, E), BF16),
            vmem((QD, C), I32),
            vmem((QD, C), F32),
            vmem((OWNERS * QD, QT, E), BF16),
            vmem((PS, PT, E), BF16),
            vmem((PS, PT, E), BF16),
            vmem((PS, E, PT), BF16),
            vmem((OWNERS, 1, ROW), I32),
            vmem((OWNERS, 1, ROW), I32),
            vmem((OWNERS, 1, ROW), F32),
            vmem((OWNERS, 1, ROW), F32),
            vmem((8, SLOTS), I32),
            pltpu.SMEM((8, SLOTS), I32),
            vmem((LINES, ROW), I32),
            vmem((LINES, ROW), F32),
            vmem((1, ROW), F32),
            vmem((CHUNKS, PT, ROW), BF16),
            vmem((CHUNKS * PER_CHUNK, QT, E), BF16),
            vmem((CHUNKS, ROW, E), BF16),
            vmem((CHUNKS, 1, ROW), F32),
            vmem((PER_CHUNK, LINES, ROW), F32),
            vmem((QD, PER_CHUNK, LINES, ROW), F32),
            vmem((2, ROW), F32),
            vmem((OWNERS, 2, ROW), F32),
            vmem((CHUNKS, SHARE, E), BF16),
            vmem((CHUNKS, 3 * SHARE, E), BF16),
            vmem(share, BF16),
            vmem(share, BF16),
            vmem(share, BF16),
            vmem(share, BF16),
            vmem(half_share, BF16),
            vmem(half_share, BF16),
            vmem(share, BF16),
            vmem(share, BF16),
            vmem(owner_block, BF16),
            vmem(owner_block, BF16),
            vmem(owner_block, BF16),
            vmem(owner_block, BF16),
            dma((8,)),
            dma,
            dma((CHIPS,)),
            dma,
            dma,
            dma,
            dma,
            dma,
            dma,
            dma,
            dma,
            dma((6 * PIECES,)),
            dma((6 * PIECES,)),
            dma,
            dma,
            dma,
            dma,
        ],
        compiler_params=pltpu.CompilerParams(collective_id=0, has_side_effects=True, vmem_limit_bytes=44 << 20),
    )(*(pltpu.with_memory_space_constraint(value, pltpu.HBM) for value in (queries, ids, teacher, passages)))


def shards(queries, passages, candidates, teacher):
    loss, grad_queries, grad_passages = step(queries.reshape(ROW, E), candidates, teacher, passages)
    loss, grad_queries, grad_passages = pl.pallas_call(
        deliver,
        out_shape=(
            jax.ShapeDtypeStruct((1, QD), F32),
            jax.ShapeDtypeStruct(grad_queries.shape, BF16),
            jax.ShapeDtypeStruct(grad_passages.shape, BF16),
        ),
        in_specs=[pl.BlockSpec(memory_space=pltpu.VMEM)] * 3,
        out_specs=(pl.BlockSpec(memory_space=pltpu.VMEM),) * 3,
        compiler_params=pltpu.CompilerParams(vmem_limit_bytes=4 << 20),
    )(loss, grad_queries, grad_passages)
    return loss.reshape(QD), grad_queries.reshape(QD, QT, E), grad_passages


def solution(mesh):
    placed = (
        P(("psg", "qry"), None, None),
        P("psg", None, None),
        P(("psg", "qry"), None),
        P(("psg", "qry"), None),
    )
    return jax.shard_map(
        shards,
        mesh=mesh,
        in_specs=placed,
        out_specs=(P(("psg", "qry")), P(("psg", "qry"), None, None), P("psg", "qry", None)),
        check_vma=False,
    )
```

```python
import math

import jax
import jax.numpy as jnp
from jax import lax
from jax.experimental import pallas as pl
from jax.experimental.pallas import tpu as pltpu
from jax.sharding import PartitionSpec as P

MESH = pl.DeviceIdType.MESH
BF16, F32, I32 = jnp.bfloat16, jnp.float32, jnp.int32
HIGHEST = lax.Precision.HIGHEST
epsilon = 1e-06
softness_scale = 0.05

OWNERS, GROUPS, CHIPS = 32, 4, 16
QD, QT, C, E, PT, PS = 4, 32, 32, 128, 256, 32
CAP = 10
ROW = QD * QT
SHARE = PT // GROUPS
PER_CHUNK = 4
CHUNKS = (OWNERS * CAP + PS * (PER_CHUNK - 1)) // PER_CHUNK
UNROLL = 8
STEPS = CHUNKS // UNROLL
WIDE = 52
TERM_WIDE = 13
EARLY_TERMS = 3
SIDE = 4
OFFSETS = sorted(
    ((dy, dz) for dy in range(SIDE) for dz in range(SIDE) if dy or dz),
    key=lambda offset: sum(min(d, SIDE - d) for d in offset),
)
LINES = 128
PIECES = 4
PIECE = PS // 2 // PIECES
SLOTS = 512
LANES_PER_SENDER = SLOTS // OWNERS
ORDER = (2, 1, 3, 0)

NT = (((1,), (1,)), ((), ()))
TN = (((0,), (0,)), ((), ()))


def iota(shape, dim):
    return lax.broadcasted_iota(I32, shape, dim)


def dot(a, b, dims=None, precision=None):
    dims = (((1,), (0,)), ((), ())) if dims is None else dims
    return lax.dot_general(a, b, dims, precision=precision, preferred_element_type=F32)


def unit_of(values):
    inverse = lax.rsqrt(jnp.sum(values * values, -1, keepdims=True) + epsilon)
    return values * inverse, inverse


def project(values, gradient):
    unit, inverse = unit_of(values)
    return inverse * (gradient - unit * jnp.sum(unit * gradient, -1, keepdims=True))


def count(mask, axis):
    return jnp.sum(jnp.where(mask, 1, 0), axis, keepdims=True)


def as_row(block):
    return jnp.concatenate([block[index : index + 1] for index in range(block.shape[0])], 1)


def same(a, b):
    return (1 - jnp.minimum((a - b) * (a - b), 1)).astype(F32)


def column_of(row):
    return jnp.broadcast_to(row, (ROW, row.shape[1])).T[:, 0:1]


def slot_tables(ids, teacher):
    lane = iota((1, ROW), 1)
    ids, teacher = as_row(ids), as_row(teacher)
    power = jnp.exp(teacher)
    same_query = (iota((ROW, ROW), 0) // C == iota((ROW, ROW), 1) // C).astype(F32)
    power_sum = dot(jnp.broadcast_to(power, (8, ROW)), same_query, precision=HIGHEST)[0:1]
    target = power / power_sum
    owner = ids >> 5
    code = (lane >> 5) * PS + (ids & (PS - 1)) + 1
    ahead = iota((ROW, ROW), 0) < iota((ROW, ROW), 1)
    rank = count((column_of(owner) == owner) & ahead, 0)
    hits = owner == iota((OWNERS, ROW), 0)
    place = iota((OWNERS, ROW), 1) & (LANES_PER_SENDER - 1)
    codes = jnp.zeros((OWNERS, ROW), I32)
    targets = jnp.zeros((OWNERS, ROW), F32)
    for slot in range(CAP):
        chosen = hits & (rank == slot)
        codes = jnp.where(place == slot, jnp.sum(jnp.where(chosen, code, 0), 1, keepdims=True), codes)
        targets = jnp.where(place == slot, jnp.sum(jnp.where(chosen, target, 0.0), 1, keepdims=True), targets)
    entropy = target * (teacher - jnp.log(power_sum))
    return codes, targets, entropy


def order_slots(codes):
    lane = iota((OWNERS, SLOTS), 1)
    mine = lane >> 4 == iota((OWNERS, SLOTS), 0)
    code = jnp.sum(jnp.where(mine, jnp.concatenate([codes] * 4, 1), 0), 0, keepdims=True) - 1
    live = code >= 0
    local = code >> 5
    query = (iota((1, SLOTS), 1) >> 4) * QD + local
    passage = jnp.where(live, code & (PS - 1), -1)
    ahead = iota((SLOTS, SLOTS), 0) < iota((SLOTS, SLOTS), 1)
    rank = count((column_of(passage) == passage) & ahead, 0)
    index = iota((PS, SLOTS), 0)
    hits = passage == index
    chunks = (count(hits, 1) + (PER_CHUNK - 1)) >> 2
    chunk_row = jnp.sum(jnp.where(lane == index, chunks, 0), 0, keepdims=True)
    first = jnp.sum(jnp.where(lane < index, chunk_row, 0), 1, keepdims=True)
    place = rank + PER_CHUNK * jnp.sum(jnp.where(hits, first, 0), 0, keepdims=True)
    place = jnp.where(live, place, -1)
    ordered = column_of(place) == iota((SLOTS, SLOTS), 1)
    ordered = jnp.sum(jnp.where(ordered, column_of(query) + 1, 0), 0, keepdims=True) - 1
    inside = (first <= lane) & (lane < first + chunks)
    chunk_passage = jnp.sum(jnp.where(inside, index, 0), 0, keepdims=True)
    last = jnp.where(lane == index, jnp.maximum(first + chunks - 1, 0), 0)
    last = jnp.where(lane == index + ROW, jnp.minimum(chunks, 1), last)
    meta = [
        jnp.maximum(ordered, 0),
        chunk_passage,
        jnp.maximum(place, 0),
        jnp.where(live, 1, 0),
        jnp.sum(last, 0, keepdims=True),
    ]
    return meta, place, query


def place_values(place, query, targets):
    mine = iota((OWNERS, SLOTS), 1) >> 4 == iota((OWNERS, SLOTS), 0)
    target = jnp.sum(jnp.where(mine, jnp.concatenate([targets] * 4, 1), 0.0), 0, keepdims=True)
    segment = iota((LINES, ROW), 1) >> 5
    query_at = jnp.full((LINES, ROW), -1, I32)
    target_at = jnp.zeros((LINES, ROW), F32)
    for slot in range(PER_CHUNK):
        chosen = place == iota((LINES, SLOTS), 0) * PER_CHUNK + slot
        found = jnp.sum(jnp.where(chosen, query + 1, 0), 1, keepdims=True) - 1
        query_at = jnp.where(segment == slot, found, query_at)
        found = jnp.sum(jnp.where(chosen, target, 0.0), 1, keepdims=True)
        target_at = jnp.where(segment == slot, found, target_at)
    return query_at, target_at


def kernel(
    q_hbm, ids_hbm, teacher_hbm, passages_hbm,
    loss_out, gq_out, gp_out,
    q_ref, ids_ref, teacher_ref,
    q_all, raw, p_norm, p_turned, code_out, code_in, target_out, target_in, meta_v, meta_s, query_at, target_at, entropy,
    weights, terms, sides, totals_at, grads, own_grads, sums_out, sums_in, part_a, part_b, r2, r1, r3, r0,
    in_left, in_right, from_left, from_right, g_sib_out, g_sib_in, g_out, g_in,
    local_sem, q_send, q_recv, relay_send, relay_recv, code_send, code_recv, target_send, target_recv,
    sums_send, sums_recv, x_send, x_recv, sib_send, sib_recv, g_send, g_recv,
):
    me = lax.axis_index("psg")
    col = lax.axis_index("qry")
    chip, core = me // 2, me % 2
    sibling = chip * 2 + (1 - core)
    right, left = (col + 1) % GROUPS, (col + GROUPS - 1) % GROUPS

    y, z = chip // SIDE, chip % SIDE

    def chip_at(dy, dz):
        return ((y + dy) % SIDE) * SIDE + (z + dz) % SIDE

    far_first = [chip_at(dy, dz) for dy, dz in reversed(OFFSETS)]
    peers = [other * 2 + side for other in far_first for side in (core, 1 - core)] + [sibling]

    small = [
        pltpu.make_async_copy(q_hbm, q_ref, local_sem.at[5]),
        pltpu.make_async_copy(ids_hbm, ids_ref, local_sem.at[6]),
        pltpu.make_async_copy(teacher_hbm, teacher_ref, local_sem.at[7]),
    ]
    for load in small:
        load.start()

    barrier = pltpu.get_barrier_semaphore()
    for other in peers:
        pl.semaphore_signal(barrier, inc=1, device_id={"psg": other}, device_id_type=MESH)
    for side in (left, right):
        pl.semaphore_signal(barrier, inc=1, device_id={"qry": side}, device_id_type=MESH)

    loads = []
    for index, relative in enumerate(ORDER):
        share = (col + relative) % GROUPS
        load = pltpu.make_async_copy(
            passages_hbm.at[:, pl.ds(pl.multiple_of(share * SHARE, SHARE), SHARE), :],
            raw.at[:, pl.ds(index * SHARE, SHARE), :],
            local_sem.at[index],
        )
        load.start()
        loads.append(load)

    small[0].wait()
    q_raw = q_ref[...].astype(F32)
    own_rows = pl.ds(me * QD, QD)
    q_all[own_rows] = unit_of(q_raw)[0].astype(BF16).reshape(QD, QT, E)
    small[1].wait()
    small[2].wait()

    codes, targets, entropy[...] = slot_tables(ids_ref[...], teacher_ref[...])
    for owner in range(OWNERS):
        code_out[owner] = codes[owner : owner + 1]
        target_out[owner] = targets[owner : owner + 1]
    code_in[me] = code_out[me]
    target_in[me] = target_out[me]
    pl.semaphore_wait(barrier, OWNERS - 1 + 2)

    for other in peers:
        pltpu.make_async_remote_copy(
            src_ref=code_out.at[other], dst_ref=code_in.at[me], send_sem=code_send, recv_sem=code_recv,
            device_id={"psg": other}, device_id_type=MESH,
        ).start()

    def send_rows(rows, sender, dy, dz):
        pltpu.make_async_remote_copy(
            src_ref=q_all.at[rows], dst_ref=q_all.at[rows], send_sem=q_send, recv_sem=q_recv.at[sender],
            device_id={"psg": chip_at(dy, dz) * 2 + core}, device_id_type=MESH,
        ).start()

    def relay(rows):
        return pltpu.make_async_remote_copy(
            src_ref=q_all.at[rows], dst_ref=q_all.at[rows], send_sem=relay_send, recv_sem=relay_recv,
            device_id={"psg": sibling}, device_id_type=MESH,
        )

    ahead = 1 + 2 * core
    back = SIDE - ahead
    for dy, dz in (
        (ahead, 0), (0, ahead), (2, 2), (ahead, ahead), (ahead, back), (back, ahead), (back, 0), (0, back), (back, back)
    ):
        send_rows(own_rows, chip, dy, dz)
    relay(own_rows).start()

    for other in peers:
        pltpu.make_async_remote_copy(
            src_ref=target_out.at[other], dst_ref=target_in.at[me], send_sem=target_send, recv_sem=target_recv,
            device_id={"psg": other}, device_id_type=MESH,
        ).start()

    for load in loads:
        load.wait()

    def normalize(begin, end):
        def run(index, carry):
            values = raw[index].astype(F32)
            unit = unit_of(values)[0].astype(BF16)
            p_norm[index] = unit
            p_turned[index] = unit.T
            return carry

        lax.fori_loop(begin, end, run, 0, unroll=4)

    def hand_on(dy, dz, along_y=False, along_z=False):
        sender = chip_at(SIDE - dy, SIDE - dz)
        rows = pl.ds((sender * 2 + core) * QD, QD)
        pltpu.make_async_copy(q_all.at[rows], q_all.at[rows], q_recv.at[sender]).wait()
        if along_y:
            send_rows(rows, sender, ahead, 0)
        if along_z:
            send_rows(rows, sender, 0, ahead)
        relay(rows).start()

    normalize(0, 32)
    hand_on(ahead, 0, along_y=True)
    hand_on(0, ahead, along_z=True)
    hand_on(ahead, ahead, True, True)
    hand_on(ahead, back, along_y=True)
    hand_on(back, ahead, along_z=True)
    hand_on(back, 0)
    hand_on(0, back)
    hand_on(back, back)
    others = pl.ds(0, OWNERS - 1)
    pltpu.make_async_copy(code_in.at[others], code_in.at[others], code_recv).wait()
    meta, place, query_of = order_slots(jnp.concatenate([code_in[owner] for owner in range(OWNERS)], 0))
    for index, row in enumerate(meta):
        meta_v[index : index + 1, :] = row
    meta_v[5:8, :] = jnp.zeros((3, SLOTS), I32)
    hand_on(2, 0)
    hand_on(0, 2)
    to_scalar = pltpu.make_async_copy(meta_v, meta_s, local_sem.at[4])
    to_scalar.start()
    for dy, dz in ((2, ahead), (2, back), (ahead, 2), (back, 2), (2, 2)):
        hand_on(dy, dz)
    pltpu.make_async_copy(target_in.at[others], target_in.at[others], target_recv).wait()
    query_at[...], target_at[...] = place_values(
        place, query_of, jnp.concatenate([target_in[owner] for owner in range(OWNERS)], 0)
    )
    to_scalar.wait()
    half = pl.ds(0, CHIPS * QD)
    pltpu.make_async_copy(q_all.at[half], q_all.at[half], relay_recv).wait()

    factor = math.log2(math.e) / softness_scale

    def gather(chunk):
        return jnp.concatenate([q_all[meta_s[0, chunk * PER_CHUNK + slot]] for slot in range(PER_CHUNK)], 0)

    def forward(step, carry):
        for inner in range(WIDE):
            chunk = step * WIDE + inner
            tokens = p_norm[meta_s[1, chunk]]
            power = jnp.exp2(dot(tokens, gather(chunk), NT) * factor)
            weights[chunk] = power.astype(BF16)
            totals_at[chunk] = jnp.sum(power, 0, keepdims=True)
        return carry

    lax.fori_loop(0, CHUNKS // WIDE, forward, 0)
    lines = [totals_at[chunk] for chunk in range(CHUNKS)] + [jnp.ones((LINES - CHUNKS, ROW), F32)]
    logs = jnp.log(jnp.concatenate(lines, 0))

    lane = iota((LINES, ROW), 1)
    same_slot = (iota((ROW, ROW), 0) >> 5 == iota((ROW, ROW), 1) >> 5).astype(F32)
    score = dot(logs, same_slot, precision=HIGHEST) * softness_scale
    power = jnp.exp(score)
    target = target_at[...]
    shown = target * score
    power_sum = jnp.zeros((1, ROW), F32)
    shown_sum = jnp.zeros((1, ROW), F32)
    for slot in range(PER_CHUNK):
        pick = slice(slot * QT, slot * QT + 1)
        belongs = query_at[:, pick] == lane
        power_sum = power_sum + jnp.sum(jnp.where(belongs, power[:, pick], 0.0), 0, keepdims=True)
        shown_sum = shown_sum + jnp.sum(jnp.where(belongs, shown[:, pick], 0.0), 0, keepdims=True)
    sums_out[0:1, :] = power_sum
    sums_out[1:2, :] = shown_sum
    sums_in[me] = sums_out[...]

    for other in peers:
        pltpu.make_async_remote_copy(
            src_ref=sums_out, dst_ref=sums_in.at[me], send_sem=sums_send, recv_sem=sums_recv,
            device_id={"psg": other}, device_id_type=MESH,
        ).start()

    def scale(chunk, carry):
        inverse = 1.0 / totals_at[chunk]
        weights[chunk] = (weights[chunk].astype(F32) * inverse).astype(BF16)
        return carry

    lax.fori_loop(0, CHUNKS, scale, 0, unroll=13)

    def query_term(step, carry):
        for inner in range(TERM_WIDE):
            chunk = step * TERM_WIDE + inner
            term = dot(p_turned[meta_s[1, chunk]], weights[chunk]).astype(BF16)
            terms[pl.ds(chunk * PER_CHUNK, PER_CHUNK)] = term.T.reshape(PER_CHUNK, QT, E)
        return carry

    lax.fori_loop(0, EARLY_TERMS, query_term, 0)

    pltpu.make_async_copy(sums_in.at[others], sums_in.at[others], sums_recv).wait()
    totals = sums_in[0]
    for owner in range(1, OWNERS):
        totals = totals + sums_in[owner]
    total_row = totals[0:1]
    slot_grads = []
    for slot in range(PER_CHUNK):
        pick = slice(slot * QT, slot * QT + 1)
        query = query_at[:, pick]
        total = jnp.sum(jnp.where(query == lane, total_row, 0.0), 1, keepdims=True)
        likelihood = power[:, pick] / jnp.where(query >= 0, total, 1.0)
        grad = jnp.where(query >= 0, likelihood - target[:, pick], 0.0)
        grads[slot] = jnp.broadcast_to(grad, (LINES, ROW))
        slot_grads.append((query & (QD - 1), grad))

    def passage_step(first, size, parts):
        def run(step, running):
            for inner in range(WIDE):
                chunk = step * WIDE + inner
                keep = same(meta_s[1, chunk], meta_s[1, jnp.maximum(chunk - 1, 0)])
                if first:
                    scale = [
                        jnp.broadcast_to(grads[slot, pl.ds(chunk, 1), :], (QT, E)) for slot in range(PER_CHUNK)
                    ]
                    side = (gather(chunk).astype(F32) * jnp.concatenate(scale, 0)).astype(BF16)
                    sides[chunk] = side
                    values = weights[chunk, 0:size]
                else:
                    side = sides[chunk]
                    values = weights[chunk, PT - size : PT]
                running = running * keep + dot(values, side)
                parts[chunk] = running.astype(BF16)
            return running

        lax.fori_loop(0, CHUNKS // WIDE, run, jnp.zeros((size, E), F32))

    def collect_one(parts, begin, out, index):
        used = meta_s[4, ROW + index].astype(F32)
        part = parts[meta_s[4, index]][begin : begin + SHARE].astype(F32) * used
        out[index] = part.astype(BF16)

    def collect(parts, begin, out):
        def run(index, carry):
            collect_one(parts, begin, out, index)
            return carry

        lax.fori_loop(0, PS, run, 0, unroll=4)

    def send_piece(kind, piece, side, source, begin, target_ref, target_begin):
        index = kind * PIECES + piece
        copy = pltpu.make_async_remote_copy(
            src_ref=source.at[pl.ds(begin + piece * PIECE, PIECE)],
            dst_ref=target_ref.at[pl.ds(target_begin + piece * PIECE, PIECE)],
            send_sem=x_send,
            recv_sem=x_recv.at[index],
            device_id={"qry": side},
            device_id_type=MESH,
        )
        copy.start()
        return copy

    def send_pieces(kind, *rest):
        return [send_piece(kind, piece, *rest) for piece in range(PIECES)]

    passage_step(True, SHARE, part_a)
    onward_right, onward_left = [], []
    for piece in range(PIECES):
        for index in range(piece * PIECE, (piece + 1) * PIECE):
            collect_one(part_a, 0, r2, index)
            collect_one(part_a, 0, r2, PS // 2 + index)
        onward_right.append(send_piece(0, piece, right, r2, 0, in_left, 0))
        onward_left.append(send_piece(1, piece, left, r2, PS // 2, in_right, 0))
    passage_step(False, 3 * SHARE, part_b)
    collect(part_b, 0, r1)
    direct_right = send_pieces(2, right, r1, PS // 2, from_left, PS // 2)
    collect(part_b, SHARE, r3)
    direct_left = send_pieces(3, left, r3, 0, from_right, 0)
    collect(part_b, 2 * SHARE, r0)

    def query_block(sender):
        sums = [jnp.zeros((QT, E), F32) for _ in range(QD)]
        for slot in range(CAP):
            place = meta_s[2, sender * LANES_PER_SENDER + slot]
            live = meta_s[3, sender * LANES_PER_SENDER + slot].astype(F32)
            term = terms[place].astype(F32) * live
            for query in range(QD):
                sums[query] = sums[query] + term * own_grads[query, place & 3, pl.ds(place >> 2, 1), :]
        return jnp.concatenate(sums, 0)

    def for_sibling(index, carry):
        g_sib_out[index] = query_block(index * 2 + (1 - core)).astype(BF16)
        return carry

    def for_chips(index, carry):
        g_out[index] = query_block(index * 2 + core).astype(BF16)
        return carry

    loss_row = jnp.log(total_row) - totals[1:2]
    one_lane = iota((1, ROW), 1)
    loss = jnp.zeros((1, ROW), F32)
    for query in range(QD):
        mine = jnp.sum(jnp.where(one_lane == me * QD + query, loss_row, 0.0), 1, keepdims=True)
        mine = mine + jnp.sum(jnp.where(one_lane >> 5 == query, entropy[...], 0.0), 1, keepdims=True)
        loss = jnp.where(one_lane == query, mine, loss)
    loss_out[...] = loss
    lax.fori_loop(EARLY_TERMS, CHUNKS // TERM_WIDE, query_term, 0)
    for slot, (local, grad) in enumerate(slot_grads):
        for query in range(QD):
            mine = jnp.where(local == query, grad, 0.0)
            own_grads[query, slot] = jnp.broadcast_to(mine, (LINES, ROW))

    for begin in range(0, CHIPS, SIDE):
        lax.fori_loop(begin, begin + SIDE, for_sibling, 0)
        blocks = pl.ds(begin, SIDE)
        pltpu.make_async_remote_copy(
            src_ref=g_sib_out.at[blocks], dst_ref=g_sib_in.at[blocks], send_sem=sib_send, recv_sem=sib_recv,
            device_id={"psg": sibling}, device_id_type=MESH,
        ).start()
    lax.fori_loop(0, CHIPS, for_chips, 0)
    pltpu.make_async_copy(g_sib_in, g_sib_in, sib_recv).wait()

    def add_sibling(index, carry):
        g_out[index] = (g_out[index].astype(F32) + g_sib_in[index].astype(F32)).astype(BF16)
        return carry

    lax.fori_loop(0, CHIPS, add_sibling, 0)

    for other in far_first:
        pltpu.make_async_remote_copy(
            src_ref=g_out.at[other], dst_ref=g_in.at[chip], send_sem=g_send, recv_sem=g_recv,
            device_id={"psg": other * 2 + core}, device_id_type=MESH,
        ).start()
    g_in[chip] = g_out[chip]

    def merge(incoming, out, begin, piece):
        for index in range(piece * PIECE, (piece + 1) * PIECE):
            both = out[begin + index].astype(F32) + incoming[index].astype(F32)
            out[begin + index] = both.astype(BF16)

    final_right, final_left = [], []
    for piece in range(PIECES):
        onward_right[piece].wait_recv()
        merge(in_left, r1, 0, piece)
        onward_left[piece].wait_recv()
        merge(in_right, r3, PS // 2, piece)
        final_right.append(send_piece(4, piece, right, r1, 0, from_left, 0))
        final_left.append(send_piece(5, piece, left, r3, PS // 2, from_right, PS // 2))

    fewer = pl.ds(0, CHIPS - 1)
    pltpu.make_async_copy(g_in.at[fewer], g_in.at[fewer], g_recv).wait()
    gradient = jnp.zeros((ROW, E), F32)
    for index in range(CHIPS):
        gradient = gradient + g_in[index].astype(F32)
    gq_out[...] = project(q_ref[...].astype(F32), gradient).astype(BF16)

    def finish(index):
        gradient = r0[index].astype(F32) + from_left[index].astype(F32) + from_right[index].astype(F32)
        values = raw[index, 3 * SHARE : 4 * SHARE, :].astype(F32)
        gp_out[index] = project(values, gradient).astype(BF16)

    for copy in (*direct_right, *direct_left):
        copy.wait_recv()
    for piece in range(PIECES):
        final_right[piece].wait_recv()
        final_left[piece].wait_recv()
        for base in (piece * PIECE, PS // 2 + piece * PIECE):
            for inner in range(PIECE):
                finish(base + inner)

    sent_pieces = pl.ds(0, 6 * PIECES)
    pltpu.make_async_copy(weights.at[sent_pieces], weights.at[sent_pieces], x_send).wait()
    pltpu.make_async_copy(g_sib_out, g_sib_out, sib_send).wait()
    pltpu.make_async_copy(code_in.at[others], code_in.at[others], code_send).wait()
    pltpu.make_async_copy(target_in.at[others], target_in.at[others], target_send).wait()
    pltpu.make_async_copy(sums_in.at[others], sums_in.at[others], sums_send).wait()
    pltpu.make_async_copy(g_in.at[fewer], g_in.at[fewer], g_send).wait()
    sent = pl.ds(0, (CHIPS - 1) * QD)
    pltpu.make_async_copy(q_all.at[sent], q_all.at[sent], q_send).wait()
    pltpu.make_async_copy(q_all.at[half], q_all.at[half], relay_send).wait()


def deliver(loss_in, gq_in, gp_in, loss_out, gq_out, gp_out):
    loss_out[...] = loss_in[:, 0:QD]
    gq_out[...] = gq_in[...]
    gp_out[...] = gp_in[...]


def step(queries, ids, teacher, passages):
    dma = pltpu.SemaphoreType.DMA
    vmem = pltpu.VMEM
    share = (PS, SHARE, E)
    half_share = (PS // 2, SHARE, E)
    owner_block = (CHIPS, ROW, E)
    return pl.pallas_call(
        kernel,
        out_shape=(
            jax.ShapeDtypeStruct((1, ROW), F32),
            jax.ShapeDtypeStruct((ROW, E), BF16),
            jax.ShapeDtypeStruct(share, BF16),
        ),
        in_specs=[pl.BlockSpec(memory_space=pltpu.HBM)] * 4,
        out_specs=(pl.BlockSpec(memory_space=pltpu.VMEM),) * 3,
        scratch_shapes=[
            vmem((ROW, E), BF16),
            vmem((QD, C), I32),
            vmem((QD, C), F32),
            vmem((OWNERS * QD, QT, E), BF16),
            vmem((PS, PT, E), BF16),
            vmem((PS, PT, E), BF16),
            vmem((PS, E, PT), BF16),
            vmem((OWNERS, 1, ROW), I32),
            vmem((OWNERS, 1, ROW), I32),
            vmem((OWNERS, 1, ROW), F32),
            vmem((OWNERS, 1, ROW), F32),
            vmem((8, SLOTS), I32),
            pltpu.SMEM((8, SLOTS), I32),
            vmem((LINES, ROW), I32),
            vmem((LINES, ROW), F32),
            vmem((1, ROW), F32),
            vmem((CHUNKS, PT, ROW), BF16),
            vmem((CHUNKS * PER_CHUNK, QT, E), BF16),
            vmem((CHUNKS, ROW, E), BF16),
            vmem((CHUNKS, 1, ROW), F32),
            vmem((PER_CHUNK, LINES, ROW), F32),
            vmem((QD, PER_CHUNK, LINES, ROW), F32),
            vmem((2, ROW), F32),
            vmem((OWNERS, 2, ROW), F32),
            vmem((CHUNKS, SHARE, E), BF16),
            vmem((CHUNKS, 3 * SHARE, E), BF16),
            vmem(share, BF16),
            vmem(share, BF16),
            vmem(share, BF16),
            vmem(share, BF16),
            vmem(half_share, BF16),
            vmem(half_share, BF16),
            vmem(share, BF16),
            vmem(share, BF16),
            vmem(owner_block, BF16),
            vmem(owner_block, BF16),
            vmem(owner_block, BF16),
            vmem(owner_block, BF16),
            dma((8,)),
            dma,
            dma((CHIPS,)),
            dma,
            dma,
            dma,
            dma,
            dma,
            dma,
            dma,
            dma,
            dma,
            dma((6 * PIECES,)),
            dma,
            dma,
            dma,
            dma,
        ],
        compiler_params=pltpu.CompilerParams(collective_id=0, has_side_effects=True, vmem_limit_bytes=44 << 20),
    )(*(pltpu.with_memory_space_constraint(value, pltpu.HBM) for value in (queries, ids, teacher, passages)))


def shards(queries, passages, candidates, teacher):
    loss, grad_queries, grad_passages = step(queries.reshape(ROW, E), candidates, teacher, passages)
    loss, grad_queries, grad_passages = pl.pallas_call(
        deliver,
        out_shape=(
            jax.ShapeDtypeStruct((1, QD), F32),
            jax.ShapeDtypeStruct(grad_queries.shape, BF16),
            jax.ShapeDtypeStruct(grad_passages.shape, BF16),
        ),
        in_specs=[pl.BlockSpec(memory_space=pltpu.VMEM)] * 3,
        out_specs=(pl.BlockSpec(memory_space=pltpu.VMEM),) * 3,
        compiler_params=pltpu.CompilerParams(vmem_limit_bytes=4 << 20),
    )(loss, grad_queries, grad_passages)
    return loss.reshape(QD), grad_queries.reshape(QD, QT, E), grad_passages


def solution(mesh):
    placed = (
        P(("psg", "qry"), None, None),
        P("psg", None, None),
        P(("psg", "qry"), None),
        P(("psg", "qry"), None),
    )
    return jax.shard_map(
        shards,
        mesh=mesh,
        in_specs=placed,
        out_specs=(P(("psg", "qry")), P(("psg", "qry"), None, None), P("psg", "qry", None)),
        check_vma=False,
    )
```

```python
import math

import jax
import jax.numpy as jnp
from jax import lax
from jax.experimental import pallas as pl
from jax.experimental.pallas import tpu as pltpu
from jax.sharding import PartitionSpec as P

MESH = pl.DeviceIdType.MESH
BF16, F32, I32 = jnp.bfloat16, jnp.float32, jnp.int32
HIGHEST = lax.Precision.HIGHEST
epsilon = 1e-06
softness_scale = 0.05

OWNERS, GROUPS, CHIPS = 32, 4, 16
QD, QT, C, E, PT, PS = 4, 32, 32, 128, 256, 32
CAP = 10
ROW = QD * QT
SHARE = PT // GROUPS
PER_CHUNK = 4
CHUNKS = (OWNERS * CAP + PS * (PER_CHUNK - 1)) // PER_CHUNK
UNROLL = 8
STEPS = CHUNKS // UNROLL
WIDE = 104
TERM_WIDE = 13
EARLY_TERMS = 3
SIDE = 4
OFFSETS = sorted(
    ((dy, dz) for dy in range(SIDE) for dz in range(SIDE) if dy or dz),
    key=lambda offset: sum(min(d, SIDE - d) for d in offset),
)
LINES = 128
PIECES = 4
PIECE = PS // 2 // PIECES
SLOTS = 512
LANES_PER_SENDER = SLOTS // OWNERS
ORDER = (2, 1, 3, 0)

NT = (((1,), (1,)), ((), ()))
TN = (((0,), (0,)), ((), ()))


def iota(shape, dim):
    return lax.broadcasted_iota(I32, shape, dim)


def dot(a, b, dims=None, precision=None):
    dims = (((1,), (0,)), ((), ())) if dims is None else dims
    return lax.dot_general(a, b, dims, precision=precision, preferred_element_type=F32)


def unit_of(values):
    inverse = lax.rsqrt(jnp.sum(values * values, -1, keepdims=True) + epsilon)
    return values * inverse, inverse


def project(values, gradient):
    unit, inverse = unit_of(values)
    return inverse * (gradient - unit * jnp.sum(unit * gradient, -1, keepdims=True))


def count(mask, axis):
    return jnp.sum(jnp.where(mask, 1, 0), axis, keepdims=True)


def as_row(block):
    return jnp.concatenate([block[index : index + 1] for index in range(block.shape[0])], 1)


def same(a, b):
    return (1 - jnp.minimum((a - b) * (a - b), 1)).astype(F32)


def column_of(row):
    return jnp.broadcast_to(row, (ROW, row.shape[1])).T[:, 0:1]


def slot_tables(ids, teacher):
    lane = iota((1, ROW), 1)
    ids, teacher = as_row(ids), as_row(teacher)
    power = jnp.exp(teacher)
    same_query = (iota((ROW, ROW), 0) // C == iota((ROW, ROW), 1) // C).astype(F32)
    power_sum = dot(jnp.broadcast_to(power, (8, ROW)), same_query, precision=HIGHEST)[0:1]
    target = power / power_sum
    owner = ids >> 5
    code = (lane >> 5) * PS + (ids & (PS - 1)) + 1
    ahead = iota((ROW, ROW), 0) < iota((ROW, ROW), 1)
    rank = count((column_of(owner) == owner) & ahead, 0)
    hits = owner == iota((OWNERS, ROW), 0)
    place = iota((OWNERS, ROW), 1) & (LANES_PER_SENDER - 1)
    codes = jnp.zeros((OWNERS, ROW), I32)
    targets = jnp.zeros((OWNERS, ROW), F32)
    for slot in range(CAP):
        chosen = hits & (rank == slot)
        codes = jnp.where(place == slot, jnp.sum(jnp.where(chosen, code, 0), 1, keepdims=True), codes)
        targets = jnp.where(place == slot, jnp.sum(jnp.where(chosen, target, 0.0), 1, keepdims=True), targets)
    entropy = target * (teacher - jnp.log(power_sum))
    return codes, targets, entropy


def order_slots(codes):
    lane = iota((OWNERS, SLOTS), 1)
    mine = lane >> 4 == iota((OWNERS, SLOTS), 0)
    code = jnp.sum(jnp.where(mine, jnp.concatenate([codes] * 4, 1), 0), 0, keepdims=True) - 1
    live = code >= 0
    local = code >> 5
    query = (iota((1, SLOTS), 1) >> 4) * QD + local
    passage = jnp.where(live, code & (PS - 1), -1)
    ahead = iota((SLOTS, SLOTS), 0) < iota((SLOTS, SLOTS), 1)
    rank = count((column_of(passage) == passage) & ahead, 0)
    index = iota((PS, SLOTS), 0)
    hits = passage == index
    chunks = (count(hits, 1) + (PER_CHUNK - 1)) >> 2
    chunk_row = jnp.sum(jnp.where(lane == index, chunks, 0), 0, keepdims=True)
    first = jnp.sum(jnp.where(lane < index, chunk_row, 0), 1, keepdims=True)
    place = rank + PER_CHUNK * jnp.sum(jnp.where(hits, first, 0), 0, keepdims=True)
    place = jnp.where(live, place, -1)
    ordered = column_of(place) == iota((SLOTS, SLOTS), 1)
    ordered = jnp.sum(jnp.where(ordered, column_of(query) + 1, 0), 0, keepdims=True) - 1
    inside = (first <= lane) & (lane < first + chunks)
    chunk_passage = jnp.sum(jnp.where(inside, index, 0), 0, keepdims=True)
    last = jnp.where(lane == index, jnp.maximum(first + chunks - 1, 0), 0)
    last = jnp.where(lane == index + ROW, jnp.minimum(chunks, 1), last)
    meta = [
        jnp.maximum(ordered, 0),
        chunk_passage,
        jnp.maximum(place, 0),
        jnp.where(live, 1, 0),
        jnp.sum(last, 0, keepdims=True),
    ]
    return meta, place, query


def place_values(place, query, targets):
    mine = iota((OWNERS, SLOTS), 1) >> 4 == iota((OWNERS, SLOTS), 0)
    target = jnp.sum(jnp.where(mine, jnp.concatenate([targets] * 4, 1), 0.0), 0, keepdims=True)
    segment = iota((LINES, ROW), 1) >> 5
    query_at = jnp.full((LINES, ROW), -1, I32)
    target_at = jnp.zeros((LINES, ROW), F32)
    for slot in range(PER_CHUNK):
        chosen = place == iota((LINES, SLOTS), 0) * PER_CHUNK + slot
        found = jnp.sum(jnp.where(chosen, query + 1, 0), 1, keepdims=True) - 1
        query_at = jnp.where(segment == slot, found, query_at)
        found = jnp.sum(jnp.where(chosen, target, 0.0), 1, keepdims=True)
        target_at = jnp.where(segment == slot, found, target_at)
    return query_at, target_at


def kernel(
    q_hbm, ids_hbm, teacher_hbm, passages_hbm,
    loss_out, gq_out, gp_out,
    q_ref, ids_ref, teacher_ref,
    q_all, raw, p_norm, p_turned, code_out, code_in, target_out, target_in, meta_v, meta_s, query_at, target_at, entropy,
    weights, terms, sides, totals_at, grads, own_grads, sums_out, sums_in, part_a, part_b, r2, r1, r3, r0,
    in_left, in_right, from_left, from_right, g_sib_out, g_sib_in, g_out, g_in,
    local_sem, q_send, q_recv, relay_send, relay_recv, code_send, code_recv, target_send, target_recv,
    sums_send, sums_recv, x_send, x_recv, sib_send, sib_recv, g_send, g_recv,
):
    me = lax.axis_index("psg")
    col = lax.axis_index("qry")
    chip, core = me // 2, me % 2
    sibling = chip * 2 + (1 - core)
    right, left = (col + 1) % GROUPS, (col + GROUPS - 1) % GROUPS

    y, z = chip // SIDE, chip % SIDE

    def chip_at(dy, dz):
        return ((y + dy) % SIDE) * SIDE + (z + dz) % SIDE

    far_first = [chip_at(dy, dz) for dy, dz in reversed(OFFSETS)]
    peers = [other * 2 + side for other in far_first for side in (core, 1 - core)] + [sibling]

    small = [
        pltpu.make_async_copy(q_hbm, q_ref, local_sem.at[5]),
        pltpu.make_async_copy(ids_hbm, ids_ref, local_sem.at[6]),
        pltpu.make_async_copy(teacher_hbm, teacher_ref, local_sem.at[7]),
    ]
    for load in small:
        load.start()

    barrier = pltpu.get_barrier_semaphore()
    for other in peers:
        pl.semaphore_signal(barrier, inc=1, device_id={"psg": other}, device_id_type=MESH)
    for side in (left, right):
        pl.semaphore_signal(barrier, inc=1, device_id={"qry": side}, device_id_type=MESH)

    loads = []
    for index, relative in enumerate(ORDER):
        share = (col + relative) % GROUPS
        load = pltpu.make_async_copy(
            passages_hbm.at[:, pl.ds(pl.multiple_of(share * SHARE, SHARE), SHARE), :],
            raw.at[:, pl.ds(index * SHARE, SHARE), :],
            local_sem.at[index],
        )
        load.start()
        loads.append(load)

    small[0].wait()
    q_raw = q_ref[...].astype(F32)
    own_rows = pl.ds(me * QD, QD)
    q_all[own_rows] = unit_of(q_raw)[0].astype(BF16).reshape(QD, QT, E)
    small[1].wait()
    small[2].wait()

    codes, targets, entropy[...] = slot_tables(ids_ref[...], teacher_ref[...])
    for owner in range(OWNERS):
        code_out[owner] = codes[owner : owner + 1]
        target_out[owner] = targets[owner : owner + 1]
    code_in[me] = code_out[me]
    target_in[me] = target_out[me]
    pl.semaphore_wait(barrier, OWNERS - 1 + 2)

    for other in peers:
        pltpu.make_async_remote_copy(
            src_ref=code_out.at[other], dst_ref=code_in.at[me], send_sem=code_send, recv_sem=code_recv,
            device_id={"psg": other}, device_id_type=MESH,
        ).start()

    def send_rows(rows, sender, dy, dz):
        pltpu.make_async_remote_copy(
            src_ref=q_all.at[rows], dst_ref=q_all.at[rows], send_sem=q_send, recv_sem=q_recv.at[sender],
            device_id={"psg": chip_at(dy, dz) * 2 + core}, device_id_type=MESH,
        ).start()

    def relay(rows):
        return pltpu.make_async_remote_copy(
            src_ref=q_all.at[rows], dst_ref=q_all.at[rows], send_sem=relay_send, recv_sem=relay_recv,
            device_id={"psg": sibling}, device_id_type=MESH,
        )

    ahead = 1 + 2 * core
    back = SIDE - ahead
    for dy, dz in (
        (ahead, 0), (0, ahead), (2, 2), (ahead, ahead), (ahead, back), (back, ahead), (back, 0), (0, back), (back, back)
    ):
        send_rows(own_rows, chip, dy, dz)
    relay(own_rows).start()

    for other in peers:
        pltpu.make_async_remote_copy(
            src_ref=target_out.at[other], dst_ref=target_in.at[me], send_sem=target_send, recv_sem=target_recv,
            device_id={"psg": other}, device_id_type=MESH,
        ).start()

    for load in loads:
        load.wait()

    def normalize(begin, end):
        def run(index, carry):
            values = raw[index].astype(F32)
            unit = unit_of(values)[0].astype(BF16)
            p_norm[index] = unit
            p_turned[index] = unit.T
            return carry

        lax.fori_loop(begin, end, run, 0, unroll=4)

    def hand_on(dy, dz, along_y=False, along_z=False):
        sender = chip_at(SIDE - dy, SIDE - dz)
        rows = pl.ds((sender * 2 + core) * QD, QD)
        pltpu.make_async_copy(q_all.at[rows], q_all.at[rows], q_recv.at[sender]).wait()
        if along_y:
            send_rows(rows, sender, ahead, 0)
        if along_z:
            send_rows(rows, sender, 0, ahead)
        relay(rows).start()

    normalize(0, 32)
    hand_on(ahead, 0, along_y=True)
    hand_on(0, ahead, along_z=True)
    hand_on(ahead, ahead, True, True)
    hand_on(ahead, back, along_y=True)
    hand_on(back, ahead, along_z=True)
    hand_on(back, 0)
    hand_on(0, back)
    hand_on(back, back)
    others = pl.ds(0, OWNERS - 1)
    pltpu.make_async_copy(code_in.at[others], code_in.at[others], code_recv).wait()
    meta, place, query_of = order_slots(jnp.concatenate([code_in[owner] for owner in range(OWNERS)], 0))
    for index, row in enumerate(meta):
        meta_v[index : index + 1, :] = row
    meta_v[5:8, :] = jnp.zeros((3, SLOTS), I32)
    hand_on(2, 0)
    hand_on(0, 2)
    to_scalar = pltpu.make_async_copy(meta_v, meta_s, local_sem.at[4])
    to_scalar.start()
    for dy, dz in ((2, ahead), (2, back), (ahead, 2), (back, 2), (2, 2)):
        hand_on(dy, dz)
    pltpu.make_async_copy(target_in.at[others], target_in.at[others], target_recv).wait()
    query_at[...], target_at[...] = place_values(
        place, query_of, jnp.concatenate([target_in[owner] for owner in range(OWNERS)], 0)
    )
    to_scalar.wait()
    half = pl.ds(0, CHIPS * QD)
    pltpu.make_async_copy(q_all.at[half], q_all.at[half], relay_recv).wait()

    factor = math.log2(math.e) / softness_scale

    def gather(chunk):
        return jnp.concatenate([q_all[meta_s[0, chunk * PER_CHUNK + slot]] for slot in range(PER_CHUNK)], 0)

    def forward(step, carry):
        for inner in range(WIDE):
            chunk = step * WIDE + inner
            tokens = p_norm[meta_s[1, chunk]]
            power = jnp.exp2(dot(tokens, gather(chunk), NT) * factor)
            weights[chunk] = power.astype(BF16)
            totals_at[chunk] = jnp.sum(power, 0, keepdims=True)
        return carry

    lax.fori_loop(0, CHUNKS // WIDE, forward, 0)
    lines = [totals_at[chunk] for chunk in range(CHUNKS)] + [jnp.ones((LINES - CHUNKS, ROW), F32)]
    logs = jnp.log(jnp.concatenate(lines, 0))

    lane = iota((LINES, ROW), 1)
    same_slot = (iota((ROW, ROW), 0) >> 5 == iota((ROW, ROW), 1) >> 5).astype(F32)
    score = dot(logs, same_slot, precision=HIGHEST) * softness_scale
    power = jnp.exp(score)
    target = target_at[...]
    shown = target * score
    power_sum = jnp.zeros((1, ROW), F32)
    shown_sum = jnp.zeros((1, ROW), F32)
    for slot in range(PER_CHUNK):
        pick = slice(slot * QT, slot * QT + 1)
        belongs = query_at[:, pick] == lane
        power_sum = power_sum + jnp.sum(jnp.where(belongs, power[:, pick], 0.0), 0, keepdims=True)
        shown_sum = shown_sum + jnp.sum(jnp.where(belongs, shown[:, pick], 0.0), 0, keepdims=True)
    sums_out[0:1, :] = power_sum
    sums_out[1:2, :] = shown_sum
    sums_in[me] = sums_out[...]

    for other in peers:
        pltpu.make_async_remote_copy(
            src_ref=sums_out, dst_ref=sums_in.at[me], send_sem=sums_send, recv_sem=sums_recv,
            device_id={"psg": other}, device_id_type=MESH,
        ).start()

    def scale(chunk, carry):
        inverse = 1.0 / totals_at[chunk]
        weights[chunk] = (weights[chunk].astype(F32) * inverse).astype(BF16)
        return carry

    lax.fori_loop(0, CHUNKS, scale, 0, unroll=13)

    def query_term(step, carry):
        for inner in range(TERM_WIDE):
            chunk = step * TERM_WIDE + inner
            term = dot(p_turned[meta_s[1, chunk]], weights[chunk]).astype(BF16)
            terms[pl.ds(chunk * PER_CHUNK, PER_CHUNK)] = term.T.reshape(PER_CHUNK, QT, E)
        return carry

    lax.fori_loop(0, EARLY_TERMS, query_term, 0)

    pltpu.make_async_copy(sums_in.at[others], sums_in.at[others], sums_recv).wait()
    totals = [sums_in[owner] for owner in range(OWNERS)]
    while len(totals) > 1:
        totals = [first + second for first, second in zip(totals[::2], totals[1::2])]
    totals = totals[0]
    total_row = totals[0:1]
    slot_grads = []
    for slot in range(PER_CHUNK):
        pick = slice(slot * QT, slot * QT + 1)
        query = query_at[:, pick]
        total = jnp.sum(jnp.where(query == lane, total_row, 0.0), 1, keepdims=True)
        likelihood = power[:, pick] / jnp.where(query >= 0, total, 1.0)
        grad = jnp.where(query >= 0, likelihood - target[:, pick], 0.0)
        grads[slot] = jnp.broadcast_to(grad, (LINES, ROW))
        slot_grads.append((query & (QD - 1), grad))

    def passage_step(first, size, parts):
        def run(step, running):
            for inner in range(WIDE):
                chunk = step * WIDE + inner
                keep = same(meta_s[1, chunk], meta_s[1, jnp.maximum(chunk - 1, 0)])
                if first:
                    scale = [
                        jnp.broadcast_to(grads[slot, pl.ds(chunk, 1), :], (QT, E)) for slot in range(PER_CHUNK)
                    ]
                    side = (gather(chunk).astype(F32) * jnp.concatenate(scale, 0)).astype(BF16)
                    sides[chunk] = side
                    values = weights[chunk, 0:size]
                else:
                    side = sides[chunk]
                    values = weights[chunk, PT - size : PT]
                running = running * keep + dot(values, side)
                parts[chunk] = running.astype(BF16)
            return running

        lax.fori_loop(0, CHUNKS // WIDE, run, jnp.zeros((size, E), F32))

    def collect_one(parts, begin, out, index):
        used = meta_s[4, ROW + index].astype(F32)
        part = parts[meta_s[4, index]][begin : begin + SHARE].astype(F32) * used
        out[index] = part.astype(BF16)

    def collect(parts, begin, out):
        def run(index, carry):
            collect_one(parts, begin, out, index)
            return carry

        lax.fori_loop(0, PS, run, 0, unroll=4)

    def send_piece(kind, piece, side, source, begin, target_ref, target_begin):
        index = kind * PIECES + piece
        copy = pltpu.make_async_remote_copy(
            src_ref=source.at[pl.ds(begin + piece * PIECE, PIECE)],
            dst_ref=target_ref.at[pl.ds(target_begin + piece * PIECE, PIECE)],
            send_sem=x_send,
            recv_sem=x_recv.at[index],
            device_id={"qry": side},
            device_id_type=MESH,
        )
        copy.start()
        return copy

    def send_pieces(kind, *rest):
        return [send_piece(kind, piece, *rest) for piece in range(PIECES)]

    passage_step(True, SHARE, part_a)
    onward_right, onward_left = [], []
    for piece in range(PIECES):
        for index in range(piece * PIECE, (piece + 1) * PIECE):
            collect_one(part_a, 0, r2, index)
            collect_one(part_a, 0, r2, PS // 2 + index)
        onward_right.append(send_piece(0, piece, right, r2, 0, in_left, 0))
        onward_left.append(send_piece(1, piece, left, r2, PS // 2, in_right, 0))
    passage_step(False, 3 * SHARE, part_b)
    collect(part_b, 0, r1)
    direct_right = send_pieces(2, right, r1, PS // 2, from_left, PS // 2)
    collect(part_b, SHARE, r3)
    direct_left = send_pieces(3, left, r3, 0, from_right, 0)
    collect(part_b, 2 * SHARE, r0)

    def query_block(sender):
        sums = [jnp.zeros((QT, E), F32) for _ in range(QD)]
        for slot in range(CAP):
            place = meta_s[2, sender * LANES_PER_SENDER + slot]
            live = meta_s[3, sender * LANES_PER_SENDER + slot].astype(F32)
            term = terms[place].astype(F32) * live
            for query in range(QD):
                sums[query] = sums[query] + term * own_grads[query, place & 3, pl.ds(place >> 2, 1), :]
        return jnp.concatenate(sums, 0)

    def for_sibling(index, carry):
        g_sib_out[index] = query_block(index * 2 + (1 - core)).astype(BF16)
        return carry

    def for_chips(index, carry):
        g_out[index] = query_block(index * 2 + core).astype(BF16)
        return carry

    loss_row = jnp.log(total_row) - totals[1:2]
    one_lane = iota((1, ROW), 1)
    loss = jnp.zeros((1, ROW), F32)
    for query in range(QD):
        mine = jnp.sum(jnp.where(one_lane == me * QD + query, loss_row, 0.0), 1, keepdims=True)
        mine = mine + jnp.sum(jnp.where(one_lane >> 5 == query, entropy[...], 0.0), 1, keepdims=True)
        loss = jnp.where(one_lane == query, mine, loss)
    loss_out[...] = loss
    lax.fori_loop(EARLY_TERMS, CHUNKS // TERM_WIDE, query_term, 0)
    for slot, (local, grad) in enumerate(slot_grads):
        for query in range(QD):
            mine = jnp.where(local == query, grad, 0.0)
            own_grads[query, slot] = jnp.broadcast_to(mine, (LINES, ROW))

    for begin in range(0, CHIPS, SIDE):
        lax.fori_loop(begin, begin + SIDE, for_sibling, 0)
        blocks = pl.ds(begin, SIDE)
        pltpu.make_async_remote_copy(
            src_ref=g_sib_out.at[blocks], dst_ref=g_sib_in.at[blocks], send_sem=sib_send, recv_sem=sib_recv,
            device_id={"psg": sibling}, device_id_type=MESH,
        ).start()
    lax.fori_loop(0, CHIPS, for_chips, 0)
    pltpu.make_async_copy(g_sib_in, g_sib_in, sib_recv).wait()

    def add_sibling(index, carry):
        g_out[index] = (g_out[index].astype(F32) + g_sib_in[index].astype(F32)).astype(BF16)
        return carry

    lax.fori_loop(0, CHIPS, add_sibling, 0)

    for other in far_first:
        pltpu.make_async_remote_copy(
            src_ref=g_out.at[other], dst_ref=g_in.at[chip], send_sem=g_send, recv_sem=g_recv,
            device_id={"psg": other * 2 + core}, device_id_type=MESH,
        ).start()
    g_in[chip] = g_out[chip]

    def merge(incoming, out, begin, piece):
        for index in range(piece * PIECE, (piece + 1) * PIECE):
            both = out[begin + index].astype(F32) + incoming[index].astype(F32)
            out[begin + index] = both.astype(BF16)

    final_right, final_left = [], []
    for piece in range(PIECES):
        onward_right[piece].wait_recv()
        merge(in_left, r1, 0, piece)
        onward_left[piece].wait_recv()
        merge(in_right, r3, PS // 2, piece)
        final_right.append(send_piece(4, piece, right, r1, 0, from_left, 0))
        final_left.append(send_piece(5, piece, left, r3, PS // 2, from_right, PS // 2))

    fewer = pl.ds(0, CHIPS - 1)
    pltpu.make_async_copy(g_in.at[fewer], g_in.at[fewer], g_recv).wait()
    gradient = jnp.zeros((ROW, E), F32)
    for index in range(CHIPS):
        gradient = gradient + g_in[index].astype(F32)
    gq_out[...] = project(q_ref[...].astype(F32), gradient).astype(BF16)

    def finish(index):
        gradient = r0[index].astype(F32) + from_left[index].astype(F32) + from_right[index].astype(F32)
        values = raw[index, 3 * SHARE : 4 * SHARE, :].astype(F32)
        gp_out[index] = project(values, gradient).astype(BF16)

    for copy in (*direct_right, *direct_left):
        copy.wait_recv()
    for piece in range(PIECES):
        final_right[piece].wait_recv()
        final_left[piece].wait_recv()
        for base in (piece * PIECE, PS // 2 + piece * PIECE):
            for inner in range(PIECE):
                finish(base + inner)

    sent_pieces = pl.ds(0, 6 * PIECES)
    pltpu.make_async_copy(weights.at[sent_pieces], weights.at[sent_pieces], x_send).wait()
    pltpu.make_async_copy(g_sib_out, g_sib_out, sib_send).wait()
    pltpu.make_async_copy(code_in.at[others], code_in.at[others], code_send).wait()
    pltpu.make_async_copy(target_in.at[others], target_in.at[others], target_send).wait()
    pltpu.make_async_copy(sums_in.at[others], sums_in.at[others], sums_send).wait()
    pltpu.make_async_copy(g_in.at[fewer], g_in.at[fewer], g_send).wait()
    sent = pl.ds(0, (CHIPS - 1) * QD)
    pltpu.make_async_copy(q_all.at[sent], q_all.at[sent], q_send).wait()
    pltpu.make_async_copy(q_all.at[half], q_all.at[half], relay_send).wait()


def deliver(loss_in, gq_in, gp_in, loss_out, gq_out, gp_out):
    loss_out[...] = loss_in[:, 0:QD]
    gq_out[...] = gq_in[...]
    gp_out[...] = gp_in[...]


def step(queries, ids, teacher, passages):
    dma = pltpu.SemaphoreType.DMA
    vmem = pltpu.VMEM
    share = (PS, SHARE, E)
    half_share = (PS // 2, SHARE, E)
    owner_block = (CHIPS, ROW, E)
    return pl.pallas_call(
        kernel,
        out_shape=(
            jax.ShapeDtypeStruct((1, ROW), F32),
            jax.ShapeDtypeStruct((ROW, E), BF16),
            jax.ShapeDtypeStruct(share, BF16),
        ),
        in_specs=[pl.BlockSpec(memory_space=pltpu.HBM)] * 4,
        out_specs=(pl.BlockSpec(memory_space=pltpu.VMEM),) * 3,
        scratch_shapes=[
            vmem((ROW, E), BF16),
            vmem((QD, C), I32),
            vmem((QD, C), F32),
            vmem((OWNERS * QD, QT, E), BF16),
            vmem((PS, PT, E), BF16),
            vmem((PS, PT, E), BF16),
            vmem((PS, E, PT), BF16),
            vmem((OWNERS, 1, ROW), I32),
            vmem((OWNERS, 1, ROW), I32),
            vmem((OWNERS, 1, ROW), F32),
            vmem((OWNERS, 1, ROW), F32),
            vmem((8, SLOTS), I32),
            pltpu.SMEM((8, SLOTS), I32),
            vmem((LINES, ROW), I32),
            vmem((LINES, ROW), F32),
            vmem((1, ROW), F32),
            vmem((CHUNKS, PT, ROW), BF16),
            vmem((CHUNKS * PER_CHUNK, QT, E), BF16),
            vmem((CHUNKS, ROW, E), BF16),
            vmem((CHUNKS, 1, ROW), F32),
            vmem((PER_CHUNK, LINES, ROW), F32),
            vmem((QD, PER_CHUNK, LINES, ROW), F32),
            vmem((2, ROW), F32),
            vmem((OWNERS, 2, ROW), F32),
            vmem((CHUNKS, SHARE, E), BF16),
            vmem((CHUNKS, 3 * SHARE, E), BF16),
            vmem(share, BF16),
            vmem(share, BF16),
            vmem(share, BF16),
            vmem(share, BF16),
            vmem(half_share, BF16),
            vmem(half_share, BF16),
            vmem(share, BF16),
            vmem(share, BF16),
            vmem(owner_block, BF16),
            vmem(owner_block, BF16),
            vmem(owner_block, BF16),
            vmem(owner_block, BF16),
            dma((8,)),
            dma,
            dma((CHIPS,)),
            dma,
            dma,
            dma,
            dma,
            dma,
            dma,
            dma,
            dma,
            dma,
            dma((6 * PIECES,)),
            dma,
            dma,
            dma,
            dma,
        ],
        compiler_params=pltpu.CompilerParams(collective_id=0, has_side_effects=True, vmem_limit_bytes=44 << 20),
    )(*(pltpu.with_memory_space_constraint(value, pltpu.HBM) for value in (queries, ids, teacher, passages)))


def shards(queries, passages, candidates, teacher):
    loss, grad_queries, grad_passages = step(queries.reshape(ROW, E), candidates, teacher, passages)
    loss, grad_queries, grad_passages = pl.pallas_call(
        deliver,
        out_shape=(
            jax.ShapeDtypeStruct((1, QD), F32),
            jax.ShapeDtypeStruct(grad_queries.shape, BF16),
            jax.ShapeDtypeStruct(grad_passages.shape, BF16),
        ),
        in_specs=[pl.BlockSpec(memory_space=pltpu.VMEM)] * 3,
        out_specs=(pl.BlockSpec(memory_space=pltpu.VMEM),) * 3,
        compiler_params=pltpu.CompilerParams(vmem_limit_bytes=4 << 20),
    )(loss, grad_queries, grad_passages)
    return loss.reshape(QD), grad_queries.reshape(QD, QT, E), grad_passages


def solution(mesh):
    placed = (
        P(("psg", "qry"), None, None),
        P("psg", None, None),
        P(("psg", "qry"), None),
        P(("psg", "qry"), None),
    )
    return jax.shard_map(
        shards,
        mesh=mesh,
        in_specs=placed,
        out_specs=(P(("psg", "qry")), P(("psg", "qry"), None, None), P("psg", "qry", None)),
        check_vma=False,
    )
```
